32 devices in a mesh: scene: 2 (over x), gx: 16 (over z, y, core).
Axes of the slice: x: 2, y: 2, z: 4, core: 2. Of those that a mesh axis runs over, the one named last changes fastest.
Arguments:
- voxels: bfloat16 [64, 128, 8, 128], P(('scene', 'gx')), parts along dimension 0, may hold values from -6 to 6
- prior: float32 [64, 128, 8], P(('scene', 'gx')), parts along dimension 0, may hold values from -6 to 410
- conv_first: bfloat16 [27, 128, 128], replicated, may hold values from -0.109375 to 0.109375
- conv_second: bfloat16 [27, 128, 128], replicated, may hold values from -0.109375 to 0.109375
- score_x: bfloat16 [128, 128], replicated, may hold values from -2 to 2
- score_y: bfloat16 [128, 128], replicated, may hold values from -1.5 to 1.5
- plane_yz_w: bfloat16 [9, 128, 128], replicated, may hold values from -0.1875 to 0.1875
- plane_xz_w: bfloat16 [9, 128, 128], replicated, may hold values from -0.1875 to 0.1875
- norm_gain: float32 [128], replicated, may hold values from 0.1 to 1.9
- mlp_in: bfloat16 [128, 512], replicated, may hold values from -0.5 to 0.5
- mlp_out: bfloat16 [512, 128], replicated, may hold values from -0.25 to 0.25
Outputs:
- encoded: bfloat16 [64, 128, 8, 128], P(('scene', 'gx')), parts along dimension 0
The draws below stay inside these ranges and needn't reach their ends.
There are 2 independent parts, one for each index of `scene`. The reference program is written for one: setup_inputs(seed, part) draws one part's arguments, and reference() takes and returns one part's arrays. A program takes and returns all parts, laid end to end along the dimension named above; an argument that names none is the same for every part. Nothing has to cross between parts.
All inputs are finite; a program needn't handle non-finite values.
Results may differ from the reference program's by a relative error of at most 0.012.
Values may be sent and summed in bfloat16 or wider, within the bound.
No kernel may reach another device: no remote copies, remote signals or barrier semaphores. Data moves between devices by JAX's collectives and lax.ppermute only.
A program may use at most 64 MiB of HBM per device.

```python
import jax
import jax.numpy as jnp
from jax import lax

C = 128
FF = 512
Y = 128
Z = 8
X = 32


def draw_prior(key, part):
    field_key = jax.random.fold_in(key, 11)
    field = jnp.clip(jax.random.normal(field_key, (X, Y, Z), jnp.float32) * 1.5, -6.0, 6.0)
    return field


def draw_voxels(key, part):
    field_key = jax.random.fold_in(key, 31)
    field = jnp.clip(jax.random.normal(field_key, (X, Y, Z, C), jnp.float32), -6.0, 6.0)
    return field.astype(jnp.bfloat16)


def draw_score_x(key, part):
    spread = float(C // 9) ** (-0.5)
    base = jax.random.normal(jax.random.fold_in(key, 41), (C, C), jnp.float32) * spread
    base = jnp.clip(base, -6.0 * spread, 6.0 * spread)
    return base.astype(jnp.bfloat16)


def bell_draw(own_key, dims, scale, most, kind=jnp.bfloat16):
    drawn = scale * jax.random.normal(own_key, dims, jnp.float32)
    return jnp.clip(drawn, min=-most, max=most).astype(kind)


def setup_inputs(seed: int = 0, part: int = 0) -> dict:
    key_of = jax.random.split(jax.random.key(seed), 12)
    part_splits = jax.random.split(jax.random.fold_in(key_of[11], part), 12)
    return {
        "voxels": draw_voxels(jax.random.fold_in(jax.random.fold_in(key_of[11], part), 71), part),
        "prior": draw_prior(jax.random.fold_in(jax.random.fold_in(key_of[11], part), 71), part),
        "conv_first": bell_draw(key_of[2], (27, C, C), (27 * C) ** -0.5, 0.109375),
        "conv_second": bell_draw(key_of[3], (27, C, C), (27 * C) ** -0.5, 0.109375),
        "score_x": draw_score_x(jax.random.fold_in(key_of[11], 71), part),
        "score_y": bell_draw(key_of[5], (C, C), (C // 9) ** -0.5, 1.5),
        "plane_yz_w": bell_draw(key_of[6], (9, C, C), (9 * C) ** -0.5, 0.1875),
        "plane_xz_w": bell_draw(key_of[7], (9, C, C), (9 * C) ** -0.5, 0.1875),
        "norm_gain": jnp.clip(1.0 + 0.18 * jax.random.normal(key_of[8], (C,), jnp.float32), 0.1, 1.9),
        "mlp_in": bell_draw(key_of[9], (C, FF), C ** -0.5, 0.5),
        "mlp_out": bell_draw(key_of[10], (FF, C), FF ** -0.5, 0.25),
    }


def activate(values):
    return jax.nn.gelu(values, approximate=True)

def volume(field, weight):
    channels = weight.shape[-1]
    kernel = weight.astype(jnp.float32).reshape(3, 3, 3, channels, channels)
    result = lax.conv_general_dilated(field.astype(jnp.float32)[None], kernel, (1, 1, 1), [(1, 1), (1, 1), (1, 1)], dimension_numbers=('NDHWC', 'DHWIO', 'NDHWC'), precision=lax.Precision.HIGHEST)
    return result[0]

def planar(field, weight):
    channels = weight.shape[-1]
    kernel = weight.astype(jnp.float32).reshape(3, 3, channels, channels)
    result = lax.conv_general_dilated(field.astype(jnp.float32)[None], kernel, (1, 1), [(1, 1), (1, 1)], dimension_numbers=('NHWC', 'HWIO', 'NHWC'), precision=lax.Precision.HIGHEST)
    return result[0]

def reference(voxels, prior, conv_first, conv_second, score_x, score_y, plane_yz_w, plane_xz_w, norm_gain, mlp_in, mlp_out):
    first = activate(volume(voxels, conv_first)).astype(jnp.bfloat16)
    feature = (volume(first, conv_second) + voxels.astype(jnp.float32)).astype(jnp.bfloat16)
    flat = feature.reshape(-1, C)
    logit_x = jnp.dot(flat, score_x, preferred_element_type=jnp.float32).reshape(feature.shape) + prior[..., None]
    logit_y = jnp.dot(flat, score_y, preferred_element_type=jnp.float32).reshape(feature.shape) + prior[..., None]
    feature_f = feature.astype(jnp.float32)
    pooled_yz = lax.optimization_barrier(jnp.sum(jax.nn.softmax(logit_x, axis=0) * feature_f, axis=0)).astype(jnp.bfloat16)
    pooled_xz = lax.optimization_barrier(jnp.sum(jax.nn.softmax(logit_y, axis=1) * feature_f, axis=1)).astype(jnp.bfloat16)
    plane_yz = planar(pooled_yz, plane_yz_w).astype(jnp.bfloat16)
    plane_xz = planar(pooled_xz, plane_xz_w).astype(jnp.bfloat16)
    joined = feature_f * (plane_yz.astype(jnp.float32)[None] + plane_xz.astype(jnp.float32)[:, None])
    scale = lax.rsqrt(lax.optimization_barrier(jnp.mean(joined * joined, axis=-1, keepdims=True)) + 1e-06)
    normed = (joined * scale * norm_gain).astype(jnp.bfloat16)
    hidden = activate(jnp.dot(normed.reshape(-1, C), mlp_in, preferred_element_type=jnp.float32)).astype(jnp.bfloat16)
    update = jnp.dot(hidden, mlp_out, preferred_element_type=jnp.float32).reshape(joined.shape)
    return (joined + update).astype(jnp.bfloat16)
```

```python
import jax
import jax.numpy as jnp
from jax import lax
from jax.sharding import PartitionSpec as P


def padded_2(shard, sides, width):
    for axis, dim in sides:
        devices, length = (lax.axis_size(axis), shard.shape[dim])
        up = [(i, (i + 1) % devices) for i in range(devices - 1)]
        down = [(j, i) for i, j in up]
        last = lax.slice_in_dim(shard, length - width, length, axis=dim)
        first = lax.slice_in_dim(shard, 0, width, axis=dim)
        before = lax.ppermute(last, axis, up)
        after = lax.ppermute(first, axis, down)
        shard = jnp.concatenate([before, shard, after], axis=dim)
    return shard


def activate(values):
    return jax.nn.gelu(values, approximate=True)


def stack_depth(field):
    depth = field.shape[-2]
    widths = [(0, 0)] * (field.ndim - 2) + [(1, 1), (0, 0)]
    padded = jnp.pad(field, widths)
    return jnp.concatenate([padded[..., shift : shift + depth, :] for shift in range(3)], axis=-1)


def volume_conv(extended, weight):
    rows = extended.shape[0] - 2
    across = extended.shape[1]
    depth = extended.shape[2]
    channels = weight.shape[-1]
    stacked = stack_depth(jnp.pad(extended, ((0, 0), (1, 1), (0, 0), (0, 0))))
    kernel = weight.reshape(3, 3, 3 * channels, channels)
    total = None
    for along_x in range(3):
        for along_y in range(3):
            window = stacked[along_x : along_x + rows, along_y : along_y + across].reshape(
                -1, 3 * channels
            )
            term = jnp.dot(window, kernel[along_x, along_y], preferred_element_type=jnp.float32)
            total = term if total is None else total + term
    return total.reshape(rows, across, depth, channels)


def plane_conv(extended, weight):
    rows = extended.shape[0] - 2
    depth = extended.shape[1]
    channels = weight.shape[-1]
    stacked = stack_depth(extended)
    kernel = weight.reshape(3, 3 * channels, channels)
    total = None
    for along in range(3):
        window = stacked[along : along + rows].reshape(-1, 3 * channels)
        term = jnp.dot(window, kernel[along], preferred_element_type=jnp.float32)
        total = term if total is None else total + term
    return total.reshape(rows, depth, channels)


def with_faces(field):
    return padded_2(field, (("gx", 0),), 1)


def swap(values, axis, mask):
    devices = lax.axis_size(axis)
    return lax.ppermute(values, axis, [(i, i ^ mask) for i in range(devices)])


def merge(own, other):
    peak, other_peak = own[0], other[0]
    top = jnp.maximum(peak, other_peak)
    top_f = top.astype(jnp.float32)
    scale = jnp.exp(peak.astype(jnp.float32) - top_f)
    other_scale = jnp.exp(other_peak.astype(jnp.float32) - top_f)
    return (
        top,
        own[1] * scale + other[1].astype(jnp.float32) * other_scale,
        own[2] * scale + other[2].astype(jnp.float32) * other_scale,
    )


def pool_over_axis(peak, norm_sum, weighted, axis):
    devices = lax.axis_size(axis)
    index = lax.axis_index(axis)
    masks = [1 << bit for bit in range(devices.bit_length() - 1)]
    parts = (peak, norm_sum, weighted)
    for mask in masks[:-1]:
        half = parts[0].shape[0] // 2
        upper = (index // mask) % 2
        kept = [lax.dynamic_slice_in_dim(p, upper * half, half, 0) for p in parts]
        sent = [lax.dynamic_slice_in_dim(p, (1 - upper) * half, half, 0) for p in parts]
        message = jnp.stack([p.astype(jnp.bfloat16) for p in sent])
        parts = merge(kept, swap(message, axis, mask))
    for mask in masks[-1:]:
        message = jnp.stack([p.astype(jnp.bfloat16) for p in parts])
        parts = merge(parts, swap(message, axis, mask))
    pooled = (parts[2] / parts[1]).astype(jnp.bfloat16)
    for mask in reversed(masks[:-1]):
        upper = (index // mask) % 2
        other = swap(pooled, axis, mask)
        pooled = jnp.where(
            upper == 1,
            jnp.concatenate([other, pooled], axis=0),
            jnp.concatenate([pooled, other], axis=0),
        )
    return pooled


def replicated_plane(pooled, weight):
    extended = jnp.pad(pooled, ((1, 1), (0, 0), (0, 0)))
    return plane_conv(extended, weight).astype(jnp.bfloat16)


def on_device(
    voxels,
    prior,
    conv_first,
    conv_second,
    score_x,
    score_y,
    plane_yz_w,
    plane_xz_w,
    norm_gain,
    mlp_in,
    mlp_out,
):
    rows, across, depth, channels = voxels.shape
    first = activate(volume_conv(with_faces(voxels), conv_first)).astype(jnp.bfloat16)
    feature_in = with_faces(first)
    feature = (volume_conv(feature_in, conv_second) + voxels.astype(jnp.float32)).astype(
        jnp.bfloat16
    )
    flat = feature.reshape(-1, channels)
    logit_x = (
        jnp.dot(flat, score_x, preferred_element_type=jnp.float32).reshape(voxels.shape)
        + prior[..., None]
    )
    logit_y = (
        jnp.dot(flat, score_y, preferred_element_type=jnp.float32).reshape(voxels.shape)
        + prior[..., None]
    )
    feature_f = feature.astype(jnp.float32)
    pooled_xz = jnp.sum(jax.nn.softmax(logit_y, axis=1) * feature_f, axis=1).astype(jnp.bfloat16)
    strip = padded_2(pooled_xz, (("gx", 0),), 1)
    plane_xz = plane_conv(strip, plane_xz_w).astype(jnp.bfloat16)
    peak = jnp.max(logit_x, axis=0)
    coarse = peak.astype(jnp.bfloat16)
    shift = jnp.exp(jnp.clip(peak - coarse.astype(jnp.float32), -60.0, 60.0))
    weights = jnp.exp(logit_x - peak) * shift
    pooled_yz = pool_over_axis(
        coarse, jnp.sum(weights, axis=0), jnp.sum(weights * feature_f, axis=0), "gx"
    )
    plane_yz = replicated_plane(pooled_yz, plane_yz_w)
    mixing = plane_yz.astype(jnp.float32)[None] + plane_xz.astype(jnp.float32)[:, None]
    joined = feature_f * mixing
    scale = lax.rsqrt(jnp.mean(joined * joined, axis=-1, keepdims=True) + 1e-06)
    normed = (joined * scale * norm_gain).astype(jnp.bfloat16)
    hidden = activate(
        jnp.dot(normed.reshape(-1, channels), mlp_in, preferred_element_type=jnp.float32)
    ).astype(jnp.bfloat16)
    update = jnp.dot(hidden, mlp_out, preferred_element_type=jnp.float32).reshape(voxels.shape)
    return (joined + update).astype(jnp.bfloat16)


def solution(mesh):
    return jax.shard_map(
        on_device,
        mesh=mesh,
        in_specs=(
            P(("scene", "gx"), None, None, None),
            P(("scene", "gx"), None, None),
            P(),
            P(),
            P(),
            P(),
            P(),
            P(),
            P(),
            P(),
            P(),
        ),
        out_specs=P(("scene", "gx"), None, None, None),
        check_vma=False,
    )
```

```python
import functools

import jax
import jax.numpy as jnp
from jax import lax
from jax.experimental import pallas as pl
from jax.experimental.pallas import tpu as pltpu
from jax.sharding import PartitionSpec as P

BF = jnp.bfloat16
F32 = jnp.float32
IN_VMEM = pl.BlockSpec(memory_space=pltpu.VMEM)


def activate(values):
    return 0.5 * values * (1.0 + jnp.tanh(0.7978845608028654 * (values + 0.044715 * values**3)))


def beside(blocks):
    return jnp.concatenate(blocks, axis=1)


def shift_depth(before, same, after, shape):
    depth = shape[1]
    place = lax.broadcasted_iota(jnp.int32, shape, 1)
    before = jnp.where(place == 0, 0.0, pltpu.roll(before.reshape(shape), 1, 1))
    after = jnp.where(place == depth - 1, 0.0, pltpu.roll(after.reshape(shape), depth - 1, 1))
    return before + same.reshape(shape) + after


def conv_pair(rows_ref, w_ref, taps, start, span):
    depth, channels = rows_ref.shape[2:]
    shape = (span, depth, channels)
    windows = [
        [rows_ref[r, pl.ds(start + b, span)].reshape(-1, channels) for b in range(3)]
        for r in range(4)
    ]
    zero = jnp.zeros((channels, channels), BF)

    def weight(a, b, c):
        return w_ref[taps[a], 3 * b + c] if 0 <= a < 3 else zero

    def product(rows, left, right):
        lhs = beside([windows[r][b] for r in rows for b in range(3)])
        rhs = jnp.concatenate(
            [
                beside([weight(r - left[0], b, left[1]), weight(r - right[0], b, right[1])])
                for r in rows
                for b in range(3)
            ],
            axis=0,
        )
        total = jnp.dot(lhs, rhs, preferred_element_type=F32)
        return total[:, :channels], total[:, channels:]

    low0, low1 = product((0, 1, 2), (0, 0), (0, 1))
    low2, high0 = product((0, 1, 2, 3), (0, 2), (1, 0))
    high1, high2 = product((1, 2, 3), (1, 1), (1, 2))
    return shift_depth(low0, low1, low2, shape), shift_depth(high0, high1, high2, shape)


def clear_ends(rows_ref):
    rows, length, depth, channels = rows_ref.shape
    blank = jnp.zeros((rows, depth, channels), rows_ref.dtype)
    rows_ref[:, 0] = blank
    rows_ref[:, length - 1] = blank


def first_kernel(axis, own_ref, near_ref, w_ref, out_ref, rows_ref):
    across = own_ref.shape[1]
    side = lax.rem(lax.axis_index(axis), 2)
    clear_ends(rows_ref)
    for row, (source, at) in enumerate(
        ((own_ref, side), (own_ref, 1 - side), (near_ref, side), (near_ref, 1 - side))
    ):
        rows_ref[row, 1 : across + 1] = source[at]
    taps = (2 * side, 1, 2 - 2 * side)
    span = across // 2
    for step in range(2):
        low, high = conv_pair(rows_ref, w_ref, taps, step * span, span)
        out_ref[0, step * span : (step + 1) * span] = activate(low).astype(BF)
        out_ref[1, step * span : (step + 1) * span] = activate(high).astype(BF)


def main_kernel(
    axis,
    first_ref,
    own_ref,
    far_ref,
    w1_ref,
    w2_ref,
    score_ref,
    prior_ref,
    feature_ref,
    message_ref,
    keep_ref,
    strip_ref,
    rows_ref,
    mid_ref,
    logit_ref,
):
    across, depth, channels = own_ref.shape[1:]
    devices = lax.axis_size(axis)
    index = lax.axis_index(axis)
    side = lax.rem(index, 2)
    clear_ends(rows_ref)
    clear_ends(mid_ref)
    for row, (source, at) in enumerate(
        ((own_ref, 1 - side), (own_ref, side), (far_ref, 1 - side), (far_ref, side))
    ):
        rows_ref[row, 1 : across + 1] = source[at]
    mid_ref[2, 1 : across + 1] = first_ref[0]
    mid_ref[3, 1 : across + 1] = first_ref[1]
    span = across // 2
    edge = jnp.logical_or(index == 0, index == devices - 1)
    inside = jnp.where(edge, 0.0, 1.0)
    for step in range(2):
        low, high = conv_pair(rows_ref, w1_ref, (2 - 2 * side, 1, 2 * side), step * span, span)
        mid_ref[1, 1 + step * span : 1 + (step + 1) * span] = activate(low).astype(BF)
        mid_ref[0, 1 + step * span : 1 + (step + 1) * span] = (activate(high) * inside).astype(BF)

    score = score_ref[...]
    tops = [None, None]
    for step in range(2):
        half = 1 - side if step == 0 else side
        start = half * span
        place = pl.ds(start, span)
        outs = conv_pair(mid_ref, w2_ref, (2 * side, 1, 2 - 2 * side), start, span)
        logits, features = [], []
        for u in range(2):
            at = side if u == 0 else 1 - side
            feature = (outs[u] + own_ref[at, place].astype(F32)).astype(BF)
            feature_ref[at, place] = feature
            both = jnp.dot(feature.reshape(-1, channels), score, preferred_element_type=F32)
            columns = prior_ref[at, half]
            prior = jnp.stack(
                [jnp.broadcast_to(columns[:, y : y + 1], (depth, channels)) for y in range(span)]
            )
            logit_y = both[:, channels:].reshape(span, depth, channels) + prior
            logit_ref[u, place] = logit_y
            top = jnp.max(logit_y, axis=0)
            tops[u] = top if tops[u] is None else jnp.maximum(tops[u], top)
            logits.append(both[:, :channels].reshape(span, depth, channels) + prior)
            features.append(feature.astype(F32))
        peak = jnp.maximum(logits[0], logits[1])
        coarse = peak.astype(BF)
        shift = jnp.exp(jnp.clip(peak - coarse.astype(F32), -60.0, 60.0))
        low, high = jnp.exp(logits[0] - peak) * shift, jnp.exp(logits[1] - peak) * shift
        parts = (coarse, low + high, low * features[0] + high * features[1])
        for k, part in enumerate(parts):
            if step == 0:
                message_ref[k * span : (k + 1) * span] = part.astype(BF)
            else:
                keep_ref[k] = part.astype(F32)
    for u in range(2):
        at = side if u == 0 else 1 - side
        weights = jnp.exp(logit_ref[u] - tops[u])
        total = jnp.sum(weights, axis=0)
        pooled = (jnp.sum(weights * feature_ref[at].astype(F32), axis=0) / total).astype(BF)
        strip_ref[u] = pooled
        message_ref[3 * span + 1 - u] = pooled


def last_kernel(
    axis,
    feature_ref,
    pooled_ref,
    strip_ref,
    yz_ref,
    xz_ref,
    gain_ref,
    in_ref,
    out_w_ref,
    out_ref,
    plane_ref,
    mix_ref,
):
    across, depth, channels = feature_ref.shape[1:]
    devices = lax.axis_size(axis)
    index = lax.axis_index(axis)
    side = lax.rem(index, 2)
    bits = devices.bit_length() - 2
    blocks = 1 << bits
    block = across // blocks
    mine = 0
    for bit in range(bits):
        mine = mine * 2 + lax.rem(index // (1 << bit), 2)
    blank = jnp.zeros((depth, channels), BF)
    plane_ref[0] = blank
    plane_ref[across + 1] = blank
    for k in range(blocks):
        place = jnp.bitwise_xor(mine, k)
        plane_ref[pl.ds(1 + place * block, block)] = pooled_ref[k * block : (k + 1) * block]

    def plane_product(windows, weights, shape):
        lhs = beside(windows)
        rhs = jnp.concatenate([beside(w) for w in weights], axis=0)
        total = jnp.dot(lhs, rhs, preferred_element_type=F32)
        parts = [total[:, c * channels : (c + 1) * channels] for c in range(3)]
        return shift_depth(*parts, shape).astype(BF).astype(F32)

    taps = (2 * side, 1, 2 - 2 * side)
    strip = strip_ref[...]
    mixed = plane_product(
        [strip[a : a + 2].reshape(-1, channels) for a in range(3)],
        [[xz_ref[taps[a], c] for c in range(3)] for a in range(3)],
        (2, depth, channels),
    )
    mix_ref[side] = mixed[0]
    mix_ref[1 - side] = mixed[1]
    gain = gain_ref[...]
    span = min(32, across)
    for step in range(across // span):
        start = step * span
        plane = plane_product(
            [plane_ref[start + b : start + b + span].reshape(-1, channels) for b in range(3)],
            [[yz_ref[b, c] for c in range(3)] for b in range(3)],
            (span, depth, channels),
        )
        for row in range(feature_ref.shape[0]):
            feature = feature_ref[row, start : start + span].astype(F32)
            joined = (feature * (plane + mix_ref[row])).reshape(-1, channels)
            mean = jnp.mean(joined * joined, axis=-1, keepdims=True)
            normed = (joined * lax.rsqrt(mean + 1e-06) * gain).astype(BF)
            hidden = activate(jnp.dot(normed, in_ref[...], preferred_element_type=F32)).astype(BF)
            update = jnp.dot(hidden, out_w_ref[...], preferred_element_type=F32)
            out_ref[row, start : start + span] = (
                (joined + update).astype(BF).reshape(span, depth, channels)
            )


def swap(values, axis, mask):
    devices = lax.axis_size(axis)
    return lax.ppermute(values, axis, [(i, i ^ mask) for i in range(devices)])


def merge(own, other):
    peak, other_peak = own[0].astype(F32), other[0].astype(F32)
    top = jnp.maximum(peak, other_peak)
    scale = jnp.exp(peak - top)
    other_scale = jnp.exp(other_peak - top)
    return (
        top,
        own[1] * scale + other[1].astype(F32) * other_scale,
        own[2] * scale + other[2].astype(F32) * other_scale,
    )


def thirds(message):
    size = (message.shape[0] - 1) // 3
    return [message[k * size : (k + 1) * size] for k in range(3)]


def kernel_call(body, outs, scratch, cost, *operands):
    return pl.pallas_call(
        body,
        out_shape=outs,
        in_specs=[IN_VMEM] * len(operands),
        out_specs=jax.tree.map(lambda _: IN_VMEM, outs),
        scratch_shapes=scratch,
        cost_estimate=pl.CostEstimate(
            flops=cost, bytes_accessed=sum(o.size * o.dtype.itemsize for o in operands), transcendentals=0
        ),
    )(*operands)


def on_device(
    axis,
    voxels,
    prior,
    conv_first,
    conv_second,
    score_x,
    score_y,
    plane_yz_w,
    plane_xz_w,
    norm_gain,
    mlp_in,
    mlp_out,
):
    rows, across, depth, channels = voxels.shape
    devices = lax.axis_size(axis)
    if rows != 2 or devices & (devices - 1) or devices < 4:
        raise ValueError("unsupported mesh")
    index = lax.axis_index(axis)
    side = index % 2
    half = across // 2
    pairs = [(i, i + 1) for i in range(1, devices - 1, 2)]
    far = lax.ppermute(voxels, axis, pairs + [(j, i) for i, j in pairs])
    near = swap(voxels, axis, 1)
    w_first = conv_first.reshape(3, 9, channels, channels)
    w_second = conv_second.reshape(3, 9, channels, channels)
    padded = (4, across + 2, depth, channels)
    field = jax.ShapeDtypeStruct(voxels.shape, BF)
    flops = 2 * voxels.size * channels * 27
    first = kernel_call(
        functools.partial(first_kernel, axis),
        field,
        [pltpu.VMEM(padded, BF)],
        flops,
        voxels,
        near,
        w_first,
    )
    score = jnp.concatenate([score_x, score_y], axis=1)
    prior_t = prior.reshape(rows, 2, half, depth).swapaxes(2, 3)
    feature, message, keep, strip = kernel_call(
        functools.partial(main_kernel, axis),
        (
            field,
            jax.ShapeDtypeStruct((3 * half + 2, depth, channels), BF),
            jax.ShapeDtypeStruct((3, half, depth, channels), F32),
            jax.ShapeDtypeStruct((2, depth, channels), BF),
        ),
        [pltpu.VMEM(padded, BF), pltpu.VMEM(padded, BF), pltpu.VMEM(voxels.shape, F32)],
        2 * flops,
        first,
        voxels,
        far,
        w_first,
        w_second,
        score,
        prior_t,
    )
    masks = [1 << bit for bit in range(devices.bit_length() - 1)]
    got = swap(message, axis, 1)
    beyond = got[3 * half]
    travel = got[3 * half + 1]
    parts = merge(keep, thirds(got[:-1]))
    neighbour = index ^ (index + 2 * side - 1)
    before = jnp.zeros((depth, channels), BF)
    for mask in masks[1:]:
        if mask != masks[-1]:
            size = parts[0].shape[0] // 2
            upper = (index // mask) % 2
            sent = [lax.dynamic_slice_in_dim(p, (1 - upper) * size, size, 0) for p in parts]
            parts = [lax.dynamic_slice_in_dim(p, upper * size, size, 0) for p in parts]
        else:
            sent = parts
        message = jnp.concatenate([p.astype(BF) for p in sent] + [travel[None]], axis=0)
        got = swap(message, axis, mask)
        travel = got[-1]
        before = jnp.where(neighbour == 2 * mask - 1, travel, before)
        parts = merge(parts, thirds(got))
    pooled = (parts[2] / parts[1]).astype(BF)
    for mask in reversed(masks[:-1]):
        pooled = jnp.concatenate([pooled, swap(pooled, axis, mask)], axis=0)
    strip = jnp.concatenate([before[None], strip, beyond[None]], axis=0)
    return kernel_call(
        functools.partial(last_kernel, axis),
        field,
        [
            pltpu.VMEM((across + 2, depth, channels), BF),
            pltpu.VMEM((rows, depth, channels), F32),
        ],
        flops // 4,
        feature,
        pooled,
        strip,
        plane_yz_w.reshape(3, 3, channels, channels),
        plane_xz_w.reshape(3, 3, channels, channels),
        norm_gain.reshape(1, channels),
        mlp_in,
        mlp_out,
    )


def solution(mesh):
    spread = ("scene", "gx")
    return jax.shard_map(
        functools.partial(on_device, "gx"),
        mesh=mesh,
        in_specs=(P(spread, None, None, None), P(spread, None, None)) + (P(),) * 9,
        out_specs=P(spread, None, None, None),
        check_vma=False,
    )
```

```python
import functools

import jax
import jax.numpy as jnp
from jax import lax
from jax.experimental import pallas as pl
from jax.experimental.pallas import tpu as pltpu
from jax.sharding import PartitionSpec as P

BF = jnp.bfloat16
F32 = jnp.float32
IN_VMEM = pl.BlockSpec(memory_space=pltpu.VMEM)
PAIR = ({0: 0, 1: 1, 2: 2}, {1: 0, 2: 1, 3: 2})
LOWER = ({0: 0, 1: 1}, {1: 0})
UPPER = ({2: 2}, {2: 1, 3: 2})


def activate(values):
    return 0.5 * values * (1.0 + jnp.tanh(0.7978845608028654 * (values + 0.044715 * values**3)))


def beside(blocks):
    return jnp.concatenate(blocks, axis=1)


def shift_depth(before, same, after, shape):
    depth = shape[1]
    place = lax.broadcasted_iota(jnp.int32, shape, 1)
    before = jnp.where(place == 0, 0.0, pltpu.roll(before.reshape(shape), 1, 1))
    after = jnp.where(place == depth - 1, 0.0, pltpu.roll(after.reshape(shape), depth - 1, 1))
    return before + same.reshape(shape) + after


def conv_rows(rows_ref, w_ref, taps, start, span, uses, names=None):
    depth, channels = rows_ref.shape[2:]
    shape = (span, depth, channels)
    zero = jnp.zeros((channels, channels), BF)
    windows = {
        r: [
            rows_ref[names[r] if names else r, pl.ds(start + b, span)].reshape(-1, channels)
            for b in range(3)
        ]
        for r in sorted(set(uses[0]) | set(uses[1]))
    }

    def weight(out, row, b, c):
        return w_ref[taps[uses[out][row]], 3 * b + c] if row in uses[out] else zero

    def product(left, right):
        rows = sorted(set(uses[left[0]]) | set(uses[right[0]]))
        lhs = beside([windows[r][b] for r in rows for b in range(3)])
        rhs = jnp.concatenate(
            [
                beside([weight(left[0], r, b, left[1]), weight(right[0], r, b, right[1])])
                for r in rows
                for b in range(3)
            ],
            axis=0,
        )
        total = jnp.dot(lhs, rhs, preferred_element_type=F32)
        return total[:, :channels], total[:, channels:]

    low0, low1 = product((0, 0), (0, 1))
    low2, high0 = product((0, 2), (1, 0))
    high1, high2 = product((1, 1), (1, 2))
    return shift_depth(low0, low1, low2, shape), shift_depth(high0, high1, high2, shape)


def clear_ends(rows_ref, width):
    rows, length, depth, channels = rows_ref.shape
    blank = jnp.zeros((width, depth, channels), rows_ref.dtype)
    for row in range(rows):
        rows_ref[row, :width] = blank
        rows_ref[row, length - width :] = blank


def first_kernel(axis, own_ref, near_ref, w1_ref, w2_ref, edge_ref, part_ref, rows_ref, mid_ref):
    across = own_ref.shape[1]
    side = lax.rem(lax.axis_index(axis), 2)
    clear_ends(rows_ref, 1)
    clear_ends(mid_ref, 1)
    clear_ends(edge_ref, 1)
    for row, (source, at) in enumerate(
        ((own_ref, side), (own_ref, 1 - side), (near_ref, side), (near_ref, 1 - side))
    ):
        rows_ref[row, 1 : across + 1] = source[at]
    taps = (2 * side, 1, 2 - 2 * side)
    back = (2 - 2 * side, 1, 2 * side)
    span = across // 2
    for step in range(2):
        start = step * span
        low, high = conv_rows(rows_ref, w1_ref, taps, start, span, PAIR)
        mid_ref[0, 1 + start : 1 + start + span] = activate(low).astype(BF)
        mid_ref[1, 1 + start : 1 + start + span] = activate(high).astype(BF)
        low, high = conv_rows(rows_ref, w1_ref, back, start, span, LOWER, {0: 1, 1: 0})
        edge_ref[0, 1 + start : 1 + start + span] = low
        edge_ref[1, 1 + start : 1 + start + span] = high
    for step in range(2):
        start = step * span
        low, high = conv_rows(mid_ref, w2_ref, taps, start, span, UPPER, {2: 0, 3: 1})
        for u, part in enumerate((low, high)):
            own = rows_ref[u, 1 + start : 1 + start + span].astype(F32)
            part_ref[u, start : start + span] = part + own


def half_kernel(axis, second, *refs):
    edge_ref, part_ref, far_ref, w1_ref, w2_ref, x_ref, y_ref, prior_ref = refs[:8]
    if second:
        state_ref, feature_ref, message_ref, keep_ref, strip_ref, rows_ref, mid_ref = refs[8:]
    else:
        feature_ref, message_ref, keep_ref, state_ref, rows_ref, mid_ref = refs[8:]
    across, depth, channels = far_ref.shape[1:]
    devices = lax.axis_size(axis)
    index = lax.axis_index(axis)
    side = lax.rem(index, 2)
    span = across // 2
    kept = lax.rem(index // 2, 2)
    half = kept if second else 1 - kept
    clear_ends(rows_ref, 2)
    inner = pl.ds(half * (span - 2), span + 2)
    local = pl.ds(2 - 2 * half, span + 2)
    rows_ref[0, local] = far_ref[1 - side, inner]
    rows_ref[1, local] = far_ref[side, inner]
    back = (2 - 2 * side, 1, 2 * side)
    low, high = conv_rows(rows_ref, w1_ref, back, 0, span + 2, UPPER, {2: 0, 3: 1})
    inside = jnp.where(jnp.logical_or(index == 0, index == devices - 1), 0.0, 1.0)
    around = pl.ds(half * span, span + 2)
    mid_ref[1] = activate(low + edge_ref[0, around]).astype(BF)
    mid_ref[0] = (activate(high + edge_ref[1, around]) * inside).astype(BF)
    blank = jnp.zeros((depth, channels), BF)
    mid_ref[0, half * (span + 1)] = blank
    mid_ref[1, half * (span + 1)] = blank
    outs = conv_rows(mid_ref, w2_ref, (2 * side, 1, 2 - 2 * side), 0, span, LOWER)
    place = pl.ds(half * span, span)
    score = beside([x_ref[...], y_ref[...]])
    logits, features = [], []
    for u in range(2):
        at = side if u == 0 else 1 - side
        feature = (outs[u] + part_ref[u, place]).astype(BF)
        feature_ref[at] = feature
        both = jnp.dot(feature.reshape(-1, channels), score, preferred_element_type=F32)
        columns = prior_ref[at, half]
        prior = jnp.stack(
            [jnp.broadcast_to(columns[:, y : y + 1], (depth, channels)) for y in range(span)]
        )
        feature = feature.astype(F32)
        features.append(feature)
        logits.append(both[:, :channels].reshape(span, depth, channels) + prior)
        logit_y = both[:, channels:].reshape(span, depth, channels) + prior
        top = jnp.max(logit_y, axis=0)
        if second:
            top = jnp.maximum(top, state_ref[u, 0])
        weights = jnp.exp(logit_y - top)
        norm_sum = jnp.sum(weights, axis=0)
        weighted = jnp.sum(weights * feature, axis=0)
        if second:
            scale = jnp.exp(state_ref[u, 0] - top)
            norm_sum = norm_sum + state_ref[u, 1] * scale
            weighted = weighted + state_ref[u, 2] * scale
            pooled = (weighted / norm_sum).astype(BF)
            strip_ref[u] = pooled
            message_ref[3 * (span // 2) + 1 - u] = pooled
        else:
            state_ref[u, 0] = top
            state_ref[u, 1] = norm_sum
            state_ref[u, 2] = weighted
    peak = jnp.maximum(logits[0], logits[1])
    coarse = peak.astype(BF)
    shift = jnp.exp(jnp.clip(peak - coarse.astype(F32), -60.0, 60.0))
    low, high = jnp.exp(logits[0] - peak) * shift, jnp.exp(logits[1] - peak) * shift
    parts = (coarse.astype(F32), low + high, low * features[0] + high * features[1])
    quarter = span // 2
    for piece in range(2):
        cut = slice(piece * quarter, (piece + 1) * quarter)

        @pl.when(side == piece)
        def _():
            for k, part in enumerate(parts):
                keep_ref[k] = part[cut]

        @pl.when(side != piece)
        def _():
            for k, part in enumerate(parts):
                message_ref[k * quarter : (k + 1) * quarter] = part[cut].astype(BF)


def last_kernel(
    axis,
    early_ref,
    late_ref,
    pooled_ref,
    strip_ref,
    yz_ref,
    xz_ref,
    gain_ref,
    in_ref,
    out_w_ref,
    out_ref,
    plane_ref,
    mix_ref,
):
    rows, half, depth, channels = early_ref.shape
    across = 2 * half
    index = lax.axis_index(axis)
    side = lax.rem(index, 2)
    kept = lax.rem(index // 2, 2)
    bits = lax.axis_size(axis).bit_length() - 2
    block = across >> bits
    order = [1, 0] + list(range(2, bits))
    mine = 0
    for bit in order:
        mine = mine * 2 + lax.rem(index // (1 << bit), 2)
    blank = jnp.zeros((depth, channels), BF)
    plane_ref[0] = blank
    plane_ref[across + 1] = blank
    for k in range(1 << bits):
        other = 0
        for bit in order:
            other = other * 2 + (k >> (bits - 1 - bit)) % 2
        place = jnp.bitwise_xor(mine, other)
        plane_ref[pl.ds(1 + place * block, block)] = pooled_ref[k * block : (k + 1) * block]

    def plane_product(windows, weights, shape):
        lhs = beside(windows)
        rhs = jnp.concatenate([beside(w) for w in weights], axis=0)
        total = jnp.dot(lhs, rhs, preferred_element_type=F32)
        parts = [total[:, c * channels : (c + 1) * channels] for c in range(3)]
        return shift_depth(*parts, shape).astype(BF).astype(F32)

    taps = (2 * side, 1, 2 - 2 * side)
    strip = strip_ref[...]
    mixed = plane_product(
        [strip[a : a + rows].reshape(-1, channels) for a in range(3)],
        [[xz_ref[taps[a], c] for c in range(3)] for a in range(3)],
        (rows, depth, channels),
    )
    mix_ref[side] = mixed[0]
    mix_ref[1 - side] = mixed[1]
    gain = gain_ref[...]
    span = min(32, half)
    for step in range(across // span):
        early = step * span < half
        feature_ref = early_ref if early else late_ref
        at = step * span % half
        start = (1 - kept if early else kept) * half + at
        plane = plane_product(
            [plane_ref[pl.ds(start + b, span)].reshape(-1, channels) for b in range(3)],
            [[yz_ref[b, c] for c in range(3)] for b in range(3)],
            (span, depth, channels),
        )
        for row in range(rows):
            feature = feature_ref[row, at : at + span].astype(F32)
            joined = (feature * (plane + mix_ref[row])).reshape(-1, channels)
            mean = jnp.mean(joined * joined, axis=-1, keepdims=True)
            normed = (joined * lax.rsqrt(mean + 1e-06) * gain).astype(BF)
            hidden = activate(jnp.dot(normed, in_ref[...], preferred_element_type=F32)).astype(BF)
            update = jnp.dot(hidden, out_w_ref[...], preferred_element_type=F32)
            out_ref[row, pl.ds(start, span)] = (
                (joined + update).astype(BF).reshape(span, depth, channels)
            )


def swap(values, axis, mask):
    devices = lax.axis_size(axis)
    return lax.ppermute(values, axis, [(i, i ^ mask) for i in range(devices)])


def merge(own, other):
    peak, other_peak = own[0], other[0].astype(F32)
    top = jnp.maximum(peak, other_peak)
    scale = jnp.exp(peak - top)
    other_scale = jnp.exp(other_peak - top)
    return [
        top,
        own[1] * scale + other[1].astype(F32) * other_scale,
        own[2] * scale + other[2].astype(F32) * other_scale,
    ]


def thirds(message):
    size = message.shape[0] // 3
    return [message[k * size : (k + 1) * size] for k in range(3)]


def kernel_call(body, outs, scratch, flops, *operands):
    moved = sum(o.size * o.dtype.itemsize for o in operands)
    return pl.pallas_call(
        body,
        out_shape=outs,
        in_specs=[IN_VMEM] * len(operands),
        out_specs=jax.tree.map(lambda _: IN_VMEM, outs),
        scratch_shapes=scratch,
        compiler_params=pltpu.CompilerParams(vmem_limit_bytes=12 * 1024 * 1024),
        cost_estimate=pl.CostEstimate(flops=flops, bytes_accessed=moved, transcendentals=0),
    )(*operands)


def on_device(
    axis,
    voxels,
    prior,
    conv_first,
    conv_second,
    score_x,
    score_y,
    plane_yz_w,
    plane_xz_w,
    norm_gain,
    mlp_in,
    mlp_out,
):
    rows, across, depth, channels = voxels.shape
    devices = lax.axis_size(axis)
    if rows != 2 or devices & (devices - 1) or devices < 8:
        raise ValueError("unsupported mesh")
    index = lax.axis_index(axis)
    half, quarter = across // 2, across // 4
    w_first = conv_first.reshape(3, 9, channels, channels)
    w_second = conv_second.reshape(3, 9, channels, channels)
    flops = 2 * voxels.size * channels * 27

    def beyond_edge(at):
        return at + 2 * (at % 2) - 1

    pairs = [(i, i + 1) for i in range(1, devices - 1, 2)]
    far = lax.ppermute(voxels, axis, pairs + [(j, i) for i, j in pairs])
    near = swap(voxels, axis, 1)
    edge, part = kernel_call(
        functools.partial(first_kernel, axis),
        (
            jax.ShapeDtypeStruct((rows, across + 2, depth, channels), F32),
            jax.ShapeDtypeStruct(voxels.shape, F32),
        ),
        [
            pltpu.VMEM((4, across + 2, depth, channels), BF),
            pltpu.VMEM((2, across + 2, depth, channels), BF),
        ],
        2 * flops,
        voxels,
        near,
        w_first,
        w_second,
    )
    prior = prior.reshape(rows, 2, half, depth).swapaxes(2, 3)

    def half_call(second, *state):
        feature = jax.ShapeDtypeStruct((rows, half, depth, channels), BF)
        message = jax.ShapeDtypeStruct((3 * quarter + 2 * second, depth, channels), BF)
        keep = jax.ShapeDtypeStruct((3, quarter, depth, channels), F32)
        last = (
            jax.ShapeDtypeStruct((rows, depth, channels), BF)
            if second
            else jax.ShapeDtypeStruct((rows, 3, depth, channels), F32)
        )
        return kernel_call(
            functools.partial(half_kernel, axis, second),
            (feature, message, keep, last),
            [
                pltpu.VMEM((2, half + 4, depth, channels), BF),
                pltpu.VMEM((2, half + 2, depth, channels), BF),
            ],
            3 * flops // 4,
            edge,
            part,
            far,
            w_first,
            w_second,
            score_x,
            score_y,
            prior,
            *state,
        )

    masks = [1 << bit for bit in range(devices.bit_length() - 1)]
    early, message, keep, state = half_call(False)
    got = swap(message, axis, masks[0])
    sent = jnp.concatenate([p.astype(BF) for p in merge(keep, thirds(got))])
    sent, state = lax.optimization_barrier((sent, state))
    arriving = swap(sent, axis, masks[1])
    late, message, keep, strip = half_call(True, state)
    got = swap(message, axis, masks[0])
    beyond = got[3 * quarter]
    carried = [got[3 * quarter + 1]]
    parts = merge(merge(keep, thirds(got[: 3 * quarter])), thirds(arriving))
    for mask in masks[2:]:
        if mask != masks[-1]:
            size = parts[0].shape[0] // 2
            upper = (index // mask) % 2
            sent = [lax.dynamic_slice_in_dim(p, (1 - upper) * size, size, 0) for p in parts]
            parts = [lax.dynamic_slice_in_dim(p, upper * size, size, 0) for p in parts]
        else:
            sent = parts
        message = jnp.concatenate([p.astype(BF) for p in sent] + [carried[-1][None]], axis=0)
        got = swap(message, axis, mask)
        carried.append(got[-1])
        last_row = carried[-1]
        parts = merge(parts, thirds(got[:-1]))
        parts[0], carried[-1] = lax.optimization_barrier((parts[0], last_row))
    pooled = (parts[2] / parts[1]).astype(BF)
    for mask in reversed(masks[2:-1]):
        pooled = jnp.concatenate([pooled, swap(pooled, axis, mask)], axis=0)
    other = index ^ masks[1]
    path = other ^ beyond_edge(other)
    row = carried[0]
    for k, value in enumerate(carried[1:]):
        row = jnp.where(path == (1 << (k + 3)) - 1, value, row)
    got = swap(jnp.concatenate([pooled, row[None]], axis=0), axis, masks[1])
    before = jnp.where((index == 0) | (index == devices - 1), jnp.zeros_like(row), got[-1])
    pooled = jnp.concatenate([pooled, got[:-1]], axis=0)
    pooled = jnp.concatenate([pooled, swap(pooled, axis, masks[0])], axis=0)
    strip = jnp.concatenate([before[None], strip, beyond[None]], axis=0)
    return kernel_call(
        functools.partial(last_kernel, axis),
        jax.ShapeDtypeStruct(voxels.shape, BF),
        [
            pltpu.VMEM((across + 2, depth, channels), BF),
            pltpu.VMEM((rows, depth, channels), F32),
        ],
        flops // 4,
        early,
        late,
        pooled,
        strip,
        plane_yz_w.reshape(3, 3, channels, channels),
        plane_xz_w.reshape(3, 3, channels, channels),
        norm_gain.reshape(1, channels),
        mlp_in,
        mlp_out,
    )


def solution(mesh):
    spread = ("scene", "gx")
    return jax.shard_map(
        functools.partial(on_device, "gx"),
        mesh=mesh,
        in_specs=(P(spread, None, None, None), P(spread, None, None)) + (P(),) * 9,
        out_specs=P(spread, None, None, None),
        check_vma=False,
    )
```

```python
import functools

import jax
import jax.numpy as jnp
from jax import lax
from jax.experimental import pallas as pl
from jax.experimental.pallas import tpu as pltpu
from jax.sharding import PartitionSpec as P

BF = jnp.bfloat16
F32 = jnp.float32
IN_VMEM = pl.BlockSpec(memory_space=pltpu.VMEM)
PAIR = ({0: 0, 1: 1, 2: 2}, {1: 0, 2: 1, 3: 2})
LOWER = ({0: 0, 1: 1}, {1: 0})
UPPER = ({2: 2}, {2: 1, 3: 2})


SLOPE = 0.7978845608028654
BEND = SLOPE * 0.044715


def twice_activate(values):
    return values + values * jnp.tanh(values * (SLOPE + BEND * (values * values)))


def activate(values):
    return 0.5 * twice_activate(values)


def beside(blocks):
    return jnp.concatenate(blocks, axis=1)


def shift_depth(before, same, after, shape):
    depth = shape[1]
    place = lax.broadcasted_iota(jnp.int32, shape, 1)
    before = jnp.where(place == 0, 0.0, pltpu.roll(before.reshape(shape), 1, 1))
    after = jnp.where(place == depth - 1, 0.0, pltpu.roll(after.reshape(shape), depth - 1, 1))
    return before + same.reshape(shape) + after


def conv_rows(rows_ref, w_ref, taps, start, span, uses, names=None):
    depth, channels = rows_ref.shape[2:]
    shape = (span, depth, channels)
    zero = jnp.zeros((channels, channels), BF)
    windows = {
        r: [
            rows_ref[names[r] if names else r, pl.ds(start + b, span)].reshape(-1, channels)
            for b in range(3)
        ]
        for r in sorted(set(uses[0]) | set(uses[1]))
    }

    def weight(out, row, b, c):
        return w_ref[taps[uses[out][row]], 3 * b + c] if row in uses[out] else zero

    def product(left, right):
        rows = sorted(set(uses[left[0]]) | set(uses[right[0]]))
        lhs = beside([windows[r][b] for r in rows for b in range(3)])
        rhs = jnp.concatenate(
            [
                beside([weight(left[0], r, b, left[1]), weight(right[0], r, b, right[1])])
                for r in rows
                for b in range(3)
            ],
            axis=0,
        )
        total = jnp.dot(lhs, rhs, preferred_element_type=F32)
        return total[:, :channels], total[:, channels:]

    low0, low1 = product((0, 0), (0, 1))
    low2, high0 = product((0, 2), (1, 0))
    high1, high2 = product((1, 1), (1, 2))
    return shift_depth(low0, low1, low2, shape), shift_depth(high0, high1, high2, shape)


def clear_ends(rows_ref, width):
    rows, length, depth, channels = rows_ref.shape
    blank = jnp.zeros((width, depth, channels), rows_ref.dtype)
    for row in range(rows):
        rows_ref[row, :width] = blank
        rows_ref[row, length - width :] = blank


def cut_kernel(axis, own_ref, first_ref, second_ref, sems):
    half = own_ref.shape[1] // 2
    kept = lax.rem(lax.axis_index(axis) // 2, 2)
    fetches = []
    for k, (at, target) in enumerate(((kept, first_ref), (1 - kept, second_ref))):
        place = pl.ds(at * (half - 2), half + 2)
        fetches.append(pltpu.make_async_copy(own_ref.at[:, place], target, sems.at[k]))
    for fetch in fetches:
        fetch.start()
    for fetch in fetches:
        fetch.wait()


def first_kernel(axis, cut0_ref, cut1_ref, near_ref, w1_ref, w2_ref, edge_ref, part_ref, rows_ref, mid_ref):
    across = near_ref.shape[1]
    span = across // 2
    index = lax.axis_index(axis)
    side = lax.rem(index, 2)
    kept = lax.rem(index // 2, 2)
    clear_ends(rows_ref, 1)
    clear_ends(mid_ref, 1)
    clear_ends(edge_ref, 1)
    for row, at in enumerate((side, 1 - side)):
        rows_ref[row, pl.ds(1 + kept * (span - 2), span + 2)] = cut0_ref[at]
        rows_ref[row, pl.ds(1 + (1 - kept) * (span - 2), span + 2)] = cut1_ref[at]
        rows_ref[2 + row, 1 : across + 1] = near_ref[at]
    taps = (2 * side, 1, 2 - 2 * side)
    back = (2 - 2 * side, 1, 2 * side)
    for step in range(2):
        start = step * span
        low, high = conv_rows(rows_ref, w1_ref, taps, start, span, PAIR)
        mid_ref[0, 1 + start : 1 + start + span] = activate(low).astype(BF)
        mid_ref[1, 1 + start : 1 + start + span] = activate(high).astype(BF)
        low, high = conv_rows(rows_ref, w1_ref, back, start, span, LOWER, {0: 1, 1: 0})
        edge_ref[0, 1 + start : 1 + start + span] = low
        edge_ref[1, 1 + start : 1 + start + span] = high
    for step in range(2):
        start = step * span
        low, high = conv_rows(mid_ref, w2_ref, taps, start, span, UPPER, {2: 0, 3: 1})
        for u, part in enumerate((low, high)):
            own = rows_ref[u, 1 + start : 1 + start + span].astype(F32)
            part_ref[u, start : start + span] = part + own


def half_kernel(axis, second, *refs):
    edge_ref, part_ref, far_ref, w1_ref, w2_ref, x_ref, y_ref, prior_ref = refs[:8]
    if second:
        state_ref, feature_ref, message_ref, keep_ref, strip_ref, rows_ref, mid_ref = refs[8:]
    else:
        feature_ref, message_ref, keep_ref, state_ref, rows_ref, mid_ref = refs[8:]
    across, depth, channels = part_ref.shape[1:]
    devices = lax.axis_size(axis)
    index = lax.axis_index(axis)
    side = lax.rem(index, 2)
    span = across // 2
    kept = lax.rem(index // 2, 2)
    half = kept if second else 1 - kept
    clear_ends(rows_ref, 2)
    local = pl.ds(2 - 2 * half, span + 2)
    border = jnp.logical_or(index == 0, index == devices - 1)
    blank = jnp.zeros((span + 2, depth, channels), BF)
    rows_ref[0, local] = jnp.where(border, blank, far_ref[1 - side])
    rows_ref[1, local] = jnp.where(border, blank, far_ref[side])
    back = (2 - 2 * side, 1, 2 * side)
    low, high = conv_rows(rows_ref, w1_ref, back, 0, span + 2, UPPER, {2: 0, 3: 1})
    inside = jnp.where(border, 0.0, 1.0)
    around = pl.ds(half * span, span + 2)
    mid_ref[1] = activate(low + edge_ref[0, around]).astype(BF)
    mid_ref[0] = (activate(high + edge_ref[1, around]) * inside).astype(BF)
    blank = jnp.zeros((depth, channels), BF)
    mid_ref[0, half * (span + 1)] = blank
    mid_ref[1, half * (span + 1)] = blank
    outs = conv_rows(mid_ref, w2_ref, (2 * side, 1, 2 - 2 * side), 0, span, LOWER)
    place = pl.ds(half * span, span)
    score = beside([x_ref[...], y_ref[...]])
    logits, features = [], []
    for u in range(2):
        at = side if u == 0 else 1 - side
        feature = (outs[u] + part_ref[u, place]).astype(BF)
        feature_ref[at] = feature
        both = jnp.dot(feature.reshape(-1, channels), score, preferred_element_type=F32)
        columns = prior_ref[at]
        columns = jnp.where(half == 0, columns[:, :span], columns[:, span:])
        prior = jnp.stack(
            [jnp.broadcast_to(columns[:, y : y + 1], (depth, channels)) for y in range(span)]
        )
        feature = feature.astype(F32)
        features.append(feature)
        logits.append(both[:, :channels].reshape(span, depth, channels) + prior)
        logit_y = both[:, channels:].reshape(span, depth, channels) + prior
        top = jnp.max(logit_y, axis=0)
        if second:
            top = jnp.maximum(top, state_ref[u, 0])
        weights = jnp.exp(logit_y - top)
        norm_sum = jnp.sum(weights, axis=0)
        weighted = jnp.sum(weights * feature, axis=0)
        if second:
            scale = jnp.exp(state_ref[u, 0] - top)
            norm_sum = norm_sum + state_ref[u, 1] * scale
            weighted = weighted + state_ref[u, 2] * scale
            pooled = (weighted / norm_sum).astype(BF)
            strip_ref[u] = pooled
            message_ref[3 * (span // 2) + 1 - u] = pooled
        else:
            state_ref[u, 0] = top
            state_ref[u, 1] = norm_sum
            state_ref[u, 2] = weighted
    peak = jnp.maximum(logits[0], logits[1])
    coarse = peak.astype(BF)
    shift = jnp.exp(jnp.clip(peak - coarse.astype(F32), -60.0, 60.0))
    low, high = jnp.exp(logits[0] - peak) * shift, jnp.exp(logits[1] - peak) * shift
    parts = (coarse.astype(F32), low + high, low * features[0] + high * features[1])
    quarter = span // 2
    for piece in range(2):
        cut = slice(piece * quarter, (piece + 1) * quarter)

        @pl.when(side == piece)
        def _():
            for k, part in enumerate(parts):
                keep_ref[k] = part[cut]

        @pl.when(side != piece)
        def _():
            for k, part in enumerate(parts):
                message_ref[k * quarter : (k + 1) * quarter] = part[cut].astype(BF)


def last_kernel(
    axis,
    early_ref,
    late_ref,
    pooled_ref,
    strip_ref,
    yz_ref,
    xz_ref,
    gain_ref,
    in_ref,
    out_w_ref,
    out_ref,
    plane_ref,
    mix_ref,
):
    rows, half, depth, channels = early_ref.shape
    across = 2 * half
    index = lax.axis_index(axis)
    side = lax.rem(index, 2)
    kept = lax.rem(index // 2, 2)
    bits = lax.axis_size(axis).bit_length() - 2
    block = across >> bits
    order = [1, 0] + list(range(2, bits))
    mine = 0
    for bit in order:
        mine = mine * 2 + lax.rem(index // (1 << bit), 2)
    blank = jnp.zeros((depth, channels), BF)
    plane_ref[0] = blank
    plane_ref[across + 1] = blank
    for k in range(1 << bits):
        other = 0
        for bit in order:
            other = other * 2 + (k >> (bits - 1 - bit)) % 2
        place = jnp.bitwise_xor(mine, other)
        plane_ref[pl.ds(1 + place * block, block)] = pooled_ref[k * block : (k + 1) * block]

    def plane_product(windows, weights, shape):
        lhs = beside(windows)
        rhs = jnp.concatenate([beside(w) for w in weights], axis=0)
        total = jnp.dot(lhs, rhs, preferred_element_type=F32)
        parts = [total[:, c * channels : (c + 1) * channels] for c in range(3)]
        return shift_depth(*parts, shape).astype(BF).astype(F32)

    taps = (2 * side, 1, 2 - 2 * side)
    strip = strip_ref[...]
    mixed = plane_product(
        [strip[a : a + rows].reshape(-1, channels) for a in range(3)],
        [[xz_ref[taps[a], c] for c in range(3)] for a in range(3)],
        (rows, depth, channels),
    )
    mix_ref[side] = mixed[0]
    mix_ref[1 - side] = mixed[1]
    gain = gain_ref[...]
    span = min(32, half)
    for step in range(across // span):
        early = step * span < half
        feature_ref = early_ref if early else late_ref
        at = step * span % half
        start = (1 - kept if early else kept) * half + at
        plane = plane_product(
            [plane_ref[pl.ds(start + b, span)].reshape(-1, channels) for b in range(3)],
            [[yz_ref[b, c] for c in range(3)] for b in range(3)],
            (span, depth, channels),
        )
        for row in range(rows):
            feature = feature_ref[row, at : at + span].astype(F32)
            joined = (feature * (plane + mix_ref[row])).reshape(-1, channels)
            mean = jnp.mean(joined * joined, axis=-1, keepdims=True)
            normed = (joined * lax.rsqrt(mean + 1e-06) * gain).astype(BF)
            hidden = jnp.dot(normed, in_ref[...], preferred_element_type=F32)
            hidden = twice_activate(hidden).astype(BF)
            update = 0.5 * jnp.dot(hidden, out_w_ref[...], preferred_element_type=F32)
            out_ref[row, pl.ds(start, span)] = (
                (joined + update).astype(BF).reshape(span, depth, channels)
            )


def swap(values, axis, mask):
    devices = lax.axis_size(axis)
    return lax.ppermute(values, axis, [(i, i ^ mask) for i in range(devices)])


def merge(own, other):
    peak, other_peak = own[0], other[0].astype(F32)
    top = jnp.maximum(peak, other_peak)
    scale = jnp.exp(peak - top)
    other_scale = jnp.exp(other_peak - top)
    return [
        top,
        own[1] * scale + other[1].astype(F32) * other_scale,
        own[2] * scale + other[2].astype(F32) * other_scale,
    ]


def thirds(message):
    size = message.shape[0] // 3
    return [message[k * size : (k + 1) * size] for k in range(3)]


def kernel_call(body, outs, scratch, flops, *operands, spaces=None):
    moved = sum(o.size * o.dtype.itemsize for o in operands)
    return pl.pallas_call(
        body,
        out_shape=outs,
        in_specs=[pl.BlockSpec(memory_space=m) for m in spaces or [pltpu.VMEM] * len(operands)],
        out_specs=jax.tree.map(lambda _: IN_VMEM, outs),
        scratch_shapes=scratch,
        compiler_params=pltpu.CompilerParams(vmem_limit_bytes=14 * 1024 * 1024),
        cost_estimate=pl.CostEstimate(flops=flops, bytes_accessed=moved, transcendentals=0),
    )(*operands)


def on_device(
    others,
    axis,
    voxels,
    prior,
    conv_first,
    conv_second,
    score_x,
    score_y,
    plane_yz_w,
    plane_xz_w,
    norm_gain,
    mlp_in,
    mlp_out,
):
    rows, across, depth, channels = voxels.shape
    devices = lax.axis_size(axis)
    if rows != 2 or devices & (devices - 1) or devices < 8:
        raise ValueError("unsupported mesh")
    index = lax.axis_index(axis)
    half, quarter = across // 2, across // 4
    w_first = conv_first.reshape(3, 9, channels, channels)
    w_second = conv_second.reshape(3, 9, channels, channels)
    flops = 2 * voxels.size * channels * 27

    def beyond_edge(at):
        return at + 2 * (at % 2) - 1

    parts = lax.axis_size(others)
    pairs = []
    for base in range(0, parts * devices, devices):
        twin = base ^ devices if (base ^ devices) < parts * devices else base
        pairs += [(base, twin), (base + devices - 1, twin + devices - 1)]
        for i in range(base + 1, base + devices - 1, 2):
            pairs += [(i, i + 1), (i + 1, i)]
    cut = jax.ShapeDtypeStruct((rows, half + 2, depth, channels), BF)
    cuts = kernel_call(
        functools.partial(cut_kernel, axis),
        (cut, cut),
        [pltpu.SemaphoreType.DMA((2,))],
        flops,
        voxels,
        spaces=(pltpu.HBM,),
    )
    far0 = lax.ppermute(cuts[0], (others, axis), pairs)
    far1 = lax.ppermute(cuts[1], (others, axis), pairs)
    near = swap(voxels, axis, 1)
    prior = prior.swapaxes(1, 2)
    edge, part = kernel_call(
        functools.partial(first_kernel, axis),
        (
            jax.ShapeDtypeStruct((rows, across + 2, depth, channels), F32),
            jax.ShapeDtypeStruct(voxels.shape, F32),
        ),
        [
            pltpu.VMEM((4, across + 2, depth, channels), BF),
            pltpu.VMEM((2, across + 2, depth, channels), BF),
        ],
        2 * flops,
        *cuts,
        near,
        w_first,
        w_second,
    )

    def half_call(second, far, *state):
        feature = jax.ShapeDtypeStruct((rows, half, depth, channels), BF)
        message = jax.ShapeDtypeStruct((3 * quarter + 2 * second, depth, channels), BF)
        keep = jax.ShapeDtypeStruct((3, quarter, depth, channels), F32)
        last = (
            jax.ShapeDtypeStruct((rows, depth, channels), BF)
            if second
            else jax.ShapeDtypeStruct((rows, 3, depth, channels), F32)
        )
        return kernel_call(
            functools.partial(half_kernel, axis, second),
            (feature, message, keep, last),
            [
                pltpu.VMEM((2, half + 4, depth, channels), BF),
                pltpu.VMEM((2, half + 2, depth, channels), BF),
            ],
            3 * flops // 4,
            edge,
            part,
            far,
            w_first,
            w_second,
            score_x,
            score_y,
            prior,
            *state,
        )

    masks = [1 << bit for bit in range(devices.bit_length() - 1)]
    early, message, keep, state = half_call(False, far0)
    got = swap(message, axis, masks[0])
    sent = jnp.concatenate([p.astype(BF) for p in merge(keep, thirds(got))])
    sent, state = lax.optimization_barrier((sent, state))
    arriving = swap(sent, axis, masks[1])
    late, message, keep, strip = half_call(True, far1, state)
    got = swap(message, axis, masks[0])
    beyond = got[3 * quarter]
    carried = [got[3 * quarter + 1]]
    parts = merge(merge(keep, thirds(got[: 3 * quarter])), thirds(arriving))
    for mask in masks[2:]:
        if mask != masks[-1]:
            size = parts[0].shape[0] // 2
            upper = (index // mask) % 2
            sent = [lax.dynamic_slice_in_dim(p, (1 - upper) * size, size, 0) for p in parts]
            parts = [lax.dynamic_slice_in_dim(p, upper * size, size, 0) for p in parts]
        else:
            sent = parts
        message = jnp.concatenate([p.astype(BF) for p in sent] + [carried[-1][None]], axis=0)
        got = swap(message, axis, mask)
        carried.append(got[-1])
        last_row = carried[-1]
        parts = merge(parts, thirds(got[:-1]))
        parts[0], carried[-1] = lax.optimization_barrier((parts[0], last_row))
    pooled = (parts[2] / parts[1]).astype(BF)
    for mask in reversed(masks[2:-1]):
        pooled = jnp.concatenate([pooled, swap(pooled, axis, mask)], axis=0)
    other = index ^ masks[1]
    path = other ^ beyond_edge(other)
    row = carried[0]
    for k, value in enumerate(carried[1:]):
        row = jnp.where(path == (1 << (k + 3)) - 1, value, row)
    got = swap(jnp.concatenate([pooled, row[None]], axis=0), axis, masks[1])
    before = jnp.where((index == 0) | (index == devices - 1), jnp.zeros_like(row), got[-1])
    pooled = jnp.concatenate([pooled, got[:-1]], axis=0)
    pooled = jnp.concatenate([pooled, swap(pooled, axis, masks[0])], axis=0)
    strip = jnp.concatenate([before[None], strip, beyond[None]], axis=0)
    return kernel_call(
        functools.partial(last_kernel, axis),
        jax.ShapeDtypeStruct(voxels.shape, BF),
        [
            pltpu.VMEM((across + 2, depth, channels), BF),
            pltpu.VMEM((rows, depth, channels), F32),
        ],
        flops // 4,
        early,
        late,
        pooled,
        strip,
        plane_yz_w.reshape(3, 3, channels, channels),
        plane_xz_w.reshape(3, 3, channels, channels),
        norm_gain.reshape(1, channels),
        mlp_in,
        mlp_out,
    )


def solution(mesh):
    spread = ("scene", "gx")
    return jax.shard_map(
        functools.partial(on_device, "scene", "gx"),
        mesh=mesh,
        in_specs=(P(spread, None, None, None), P(spread, None, None)) + (P(),) * 9,
        out_specs=P(spread, None, None, None),
        check_vma=False,
    )
```

```python
import functools

import jax
import jax.numpy as jnp
from jax import lax
from jax.experimental import pallas as pl
from jax.experimental.pallas import tpu as pltpu
from jax.sharding import PartitionSpec as P

BF = jnp.bfloat16
F32 = jnp.float32
PAIR = ({0: 0, 1: 1, 2: 2}, {1: 0, 2: 1, 3: 2})
LOWER = ({0: 0, 1: 1}, {1: 0})
UPPER = ({2: 2}, {2: 1, 3: 2})


SLOPE = 0.7978845608028654
BEND = SLOPE * 0.044715


def twice_activate(values):
    return values + values * jnp.tanh(values * (SLOPE + BEND * (values * values)))


def activate(values):
    return 0.5 * twice_activate(values)


def beside(blocks):
    return jnp.concatenate(blocks, axis=1)


def shift_depth(before, same, after, shape):
    depth = shape[1]
    place = lax.broadcasted_iota(jnp.int32, shape, 1)
    before = jnp.where(place == 0, 0.0, pltpu.roll(before.reshape(shape), 1, 1))
    after = jnp.where(place == depth - 1, 0.0, pltpu.roll(after.reshape(shape), depth - 1, 1))
    return before + same.reshape(shape) + after


def conv_rows(window, w_ref, taps, shape, uses):
    channels = shape[-1]
    zero = jnp.zeros((channels, channels), BF)
    windows = {r: [window(r, b) for b in range(3)] for r in sorted(set(uses[0]) | set(uses[1]))}

    def weight(out, row, b, c):
        return w_ref[taps[uses[out][row]], 3 * b + c] if row in uses[out] else zero

    def product(left, right):
        rows = sorted(set(uses[left[0]]) | set(uses[right[0]]))
        lhs = beside([windows[r][b] for r in rows for b in range(3)])
        rhs = jnp.concatenate(
            [
                beside([weight(left[0], r, b, left[1]), weight(right[0], r, b, right[1])])
                for r in rows
                for b in range(3)
            ],
            axis=0,
        )
        total = jnp.dot(lhs, rhs, preferred_element_type=F32)
        return total[:, :channels], total[:, channels:]

    low0, low1 = product((0, 0), (0, 1))
    low2, high0 = product((0, 2), (1, 0))
    high1, high2 = product((1, 1), (1, 2))
    return shift_depth(low0, low1, low2, shape), shift_depth(high0, high1, high2, shape)


def clear_ends(rows_ref, width):
    rows, length, depth, channels = rows_ref.shape
    blank = jnp.zeros((width, depth, channels), rows_ref.dtype)
    for row in range(rows):
        rows_ref[row, :width] = blank
        rows_ref[row, length - width :] = blank


def bit_of(index, bit):
    return lax.rem(index // (1 << bit), 2)


def pieces_of(index, second):
    flip = 0 if second else 1
    return [2 * jnp.bitwise_xor(bit_of(index, 1 + k), flip) + k for k in range(2)]


def clamp(start, across, length):
    return jnp.clip(start, 0, across - length)


def cut_kernel(axis, own_ref, early_ref, late_ref, sems):
    across = own_ref.shape[1]
    quarter, length = across // 4, early_ref.shape[2]
    devices = lax.axis_size(axis)
    index = lax.axis_index(axis)
    taker = lax.rem(index + 2 * lax.rem(index, 2) - 1 + devices, devices)
    fetches = []
    for k, target in enumerate((early_ref, late_ref)):
        for p, piece in enumerate(pieces_of(taker, k == 1)):
            place = pl.ds(clamp(piece * quarter - 2, across, length), length)
            fetches.append(
                pltpu.make_async_copy(own_ref.at[:, place], target.at[:, p], sems.at[k, p])
            )
    for fetch in fetches:
        fetch.start()
    for fetch in fetches:
        fetch.wait()


def first_kernel(axis, own_ref, near_ref, w1_ref, w2_ref, edge_ref, part_ref, rows_ref, mid_ref):
    across, depth, channels = own_ref.shape[1:]
    span = across // 2
    shape = (span, depth, channels)
    side = lax.rem(lax.axis_index(axis), 2)
    clear_ends(rows_ref, 1)
    clear_ends(mid_ref, 1)
    clear_ends(edge_ref, 1)
    for row, at in enumerate((side, 1 - side)):
        rows_ref[row, 1 : across + 1] = own_ref[at]
        rows_ref[2 + row, 1 : across + 1] = near_ref[at]
    taps = (2 * side, 1, 2 - 2 * side)
    back = (2 - 2 * side, 1, 2 * side)

    def windows(ref, names, start):
        def window(r, b):
            return ref[names[r], start + b : start + b + span].reshape(-1, channels)

        return window

    for step in range(2):
        start = step * span
        inner = slice(1 + start, 1 + start + span)
        low, high = conv_rows(windows(rows_ref, range(4), start), w1_ref, taps, shape, PAIR)
        mid_ref[0, inner] = activate(low).astype(BF)
        mid_ref[1, inner] = activate(high).astype(BF)
        low, high = conv_rows(windows(rows_ref, (1, 0), start), w1_ref, back, shape, LOWER)
        edge_ref[0, inner] = low
        edge_ref[1, inner] = high
    for step in range(2):
        start = step * span
        outs = conv_rows(windows(mid_ref, {2: 0, 3: 1}, start), w2_ref, taps, shape, UPPER)
        for u in range(2):
            own = rows_ref[u, 1 + start : 1 + start + span].astype(F32)
            part_ref[u, start : start + span] = outs[u] + own


def half_kernel(axis, second, *refs):
    edge_ref, part_ref, far_ref, w1_ref, w2_ref, x_ref, y_ref, prior_ref = refs[:8]
    if second:
        early_ref, feature_ref, message_ref, keep_ref, strip_ref, rows_ref, mid_ref = refs[8:]
    else:
        feature_ref, message_ref, keep_ref, rows_ref, mid_ref = refs[8:]
    across, depth, channels = part_ref.shape[1:]
    quarter, length = across // 4, far_ref.shape[2]
    span = 2 * quarter
    devices = lax.axis_size(axis)
    index = lax.axis_index(axis)
    side = lax.rem(index, 2)
    pieces = pieces_of(index, second)
    border = jnp.logical_or(index == 0, index == devices - 1)
    inside = jnp.where(border, 0.0, 1.0)
    blank = jnp.zeros((4, depth, channels), BF)
    absent = jnp.zeros((length, depth, channels), BF)
    for p, piece in enumerate(pieces):
        start = piece * quarter - 2
        place = pl.ds(2 + clamp(start, across, length) - start, length)
        for row, at in enumerate((1 - side, side)):
            rows_ref[row, p, :4] = blank
            rows_ref[row, p, length:] = blank
            rows_ref[row, p, place] = jnp.where(border, absent, far_ref[at, p])

    def windows(ref, names, start, rows):
        def window(r, b):
            return jnp.concatenate(
                [ref[names[r], p, start + b : start + b + rows].reshape(-1, channels) for p in range(2)]
            )

        return window

    around = quarter + 2
    back = (2 - 2 * side, 1, 2 * side)
    far_rows = windows(rows_ref, {2: 0, 3: 1}, 2, around)
    low, high = conv_rows(far_rows, w1_ref, back, (2 * around, depth, channels), UPPER)
    for p, piece in enumerate(pieces):
        cut = slice(p * around, (p + 1) * around)
        place = pl.ds(piece * quarter, around)
        mid_ref[1, p] = activate(low[cut] + edge_ref[0, place]).astype(BF)
        mid_ref[0, p] = (activate(high[cut] + edge_ref[1, place]) * inside).astype(BF)
        outside = 0 if p == 0 else around - 1

        @pl.when(piece == 3 * p)
        def _():
            mid_ref[0, p, outside] = blank[0]
            mid_ref[1, p, outside] = blank[0]

    taps = (2 * side, 1, 2 - 2 * side)
    mid_rows = windows(mid_ref, range(2), 0, quarter)
    outs = conv_rows(mid_rows, w2_ref, taps, (span, depth, channels), LOWER)
    across_score, along_score = x_ref[...], y_ref[...]

    def prior_of(at, pieces):
        table = prior_ref[at]
        columns = []
        for p, piece in enumerate(pieces):
            low, high = (table[:, k * quarter : (k + 1) * quarter] for k in (p, 2 + p))
            both = jnp.where(piece == p, low, high)
            columns += [
                jnp.broadcast_to(both[:, y : y + 1], (depth, channels)) for y in range(quarter)
            ]
        return jnp.stack(columns)

    logits, features = [], []
    for u in range(2):
        at = side if u == 0 else 1 - side
        part = jnp.concatenate([part_ref[u, pl.ds(piece * quarter, quarter)] for piece in pieces])
        feature = (outs[u] + part).astype(BF)
        feature_ref[at] = feature
        prior = prior_of(at, pieces)
        if not second:
            logit = jnp.dot(feature.reshape(-1, channels), across_score, preferred_element_type=F32)
        else:
            score = beside([across_score, along_score])
            both = jnp.dot(feature.reshape(-1, channels), score, preferred_element_type=F32)
            logit = both[:, :channels]
            logit_y = both[:, channels:].reshape(span, depth, channels) + prior
            other = early_ref[at]
            other_y = jnp.dot(other.reshape(-1, channels), along_score, preferred_element_type=F32)
            other_y = other_y.reshape(span, depth, channels) + prior_of(at, pieces_of(index, False))
            top = jnp.maximum(jnp.max(logit_y, axis=0), jnp.max(other_y, axis=0))
            weights, others = jnp.exp(logit_y - top), jnp.exp(other_y - top)
            norm_sum = jnp.sum(weights, axis=0) + jnp.sum(others, axis=0)
            weighted = jnp.sum(weights * feature.astype(F32), axis=0)
            weighted = weighted + jnp.sum(others * other.astype(F32), axis=0)
            pooled = (weighted / norm_sum).astype(BF)
            strip_ref[u] = pooled
            message_ref[3 * quarter + 1 - u] = pooled
        features.append(feature.astype(F32))
        logits.append(logit.reshape(span, depth, channels) + prior)
    peak = jnp.maximum(logits[0], logits[1])
    coarse = peak.astype(BF)
    shift = jnp.exp(jnp.clip(peak - coarse.astype(F32), -60.0, 60.0))
    low, high = jnp.exp(logits[0] - peak) * shift, jnp.exp(logits[1] - peak) * shift
    parts = (coarse.astype(F32), low + high, low * features[0] + high * features[1])
    for p in range(2):
        cut = slice(p * quarter, (p + 1) * quarter)

        @pl.when(side == p)
        def _():
            for k, part in enumerate(parts):
                keep_ref[k] = part[cut]

        @pl.when(side != p)
        def _():
            for k, part in enumerate(parts):
                message_ref[k * quarter : (k + 1) * quarter] = part[cut].astype(BF)


def last_kernel(
    axis,
    early_ref,
    late_ref,
    pooled_ref,
    strip_ref,
    yz_ref,
    xz_ref,
    gain_ref,
    in_ref,
    out_w_ref,
    out_hbm,
    plane_ref,
    mix_ref,
    out_ref,
    sems,
):
    rows, span, depth, channels = early_ref.shape
    across, quarter = 2 * span, span // 2
    index = lax.axis_index(axis)
    side = lax.rem(index, 2)
    bits = lax.axis_size(axis).bit_length() - 2
    block = across >> bits
    blank = jnp.zeros((depth, channels), BF)
    plane_ref[0] = blank
    plane_ref[across + 1] = blank
    for k in range(1 << bits):
        flips = [(k >> (bits - 1 - b)) % 2 for b in range(bits)]
        core = jnp.bitwise_xor(side, flips[0])
        ahead = jnp.where(core == 0, bit_of(index, 1), bit_of(index, 2))
        after = jnp.where(core == 0, bit_of(index, 2), bit_of(index, 1))
        place = 2 * jnp.bitwise_xor(ahead, flips[1]) + core
        place = 2 * place + jnp.bitwise_xor(after, flips[2])
        for b in range(3, bits):
            place = 2 * place + jnp.bitwise_xor(bit_of(index, b), flips[b])
        plane_ref[pl.ds(1 + place * block, block)] = pooled_ref[k * block : (k + 1) * block]

    def plane_product(windows, weights, shape):
        lhs = beside(windows)
        rhs = jnp.concatenate([beside(w) for w in weights], axis=0)
        total = jnp.dot(lhs, rhs, preferred_element_type=F32)
        parts = [total[:, c * channels : (c + 1) * channels] for c in range(3)]
        return shift_depth(*parts, shape).astype(BF).astype(F32)

    taps = (2 * side, 1, 2 - 2 * side)
    strip = strip_ref[...]
    mixed = plane_product(
        [strip[a : a + rows].reshape(-1, channels) for a in range(3)],
        [[xz_ref[taps[a], c] for c in range(3)] for a in range(3)],
        (rows, depth, channels),
    )
    mix_ref[side] = mixed[0]
    mix_ref[1 - side] = mixed[1]
    gain = gain_ref[...]
    copies = []
    for step, feature_ref in enumerate((early_ref, late_ref)):
        starts = [piece * quarter for piece in pieces_of(index, step == 1)]
        plane = plane_product(
            [
                jnp.concatenate(
                    [plane_ref[pl.ds(at + b, quarter)].reshape(-1, channels) for at in starts]
                )
                for b in range(3)
            ],
            [[yz_ref[b, c] for c in range(3)] for b in range(3)],
            (span, depth, channels),
        )
        mixing = plane[None] + jnp.stack([mix_ref[row] for row in range(rows)])[:, None]
        joined = (feature_ref[...].astype(F32) * mixing).reshape(-1, channels)
        mean = jnp.mean(joined * joined, axis=-1, keepdims=True)
        normed = (joined * lax.rsqrt(mean + 1e-06) * gain).astype(BF)
        hidden = jnp.dot(normed, in_ref[...], preferred_element_type=F32)
        hidden = twice_activate(hidden).astype(BF)
        update = 0.5 * jnp.dot(hidden, out_w_ref[...], preferred_element_type=F32)
        encoded = (joined + update).astype(BF).reshape(rows, 2, quarter, depth, channels)
        for row in range(rows):
            for p, at in enumerate(starts):
                slot = 2 * step + p
                out_ref[row, slot] = encoded[row, p]
                copies.append(
                    pltpu.make_async_copy(
                        out_ref.at[row, slot],
                        out_hbm.at[row, pl.ds(at, quarter)],
                        sems.at[row, slot],
                    )
                )
                copies[-1].start()
    for copy in copies:
        copy.wait()


def swap(values, axis, mask, odd_mask=None):
    masks = (mask, mask if odd_mask is None else odd_mask)
    devices = lax.axis_size(axis)
    return lax.ppermute(values, axis, [(i, i ^ masks[i % 2]) for i in range(devices)])


def merge(own, other):
    peak, other_peak = own[0], other[0].astype(F32)
    top = jnp.maximum(peak, other_peak)
    scale = jnp.exp(peak - top)
    other_scale = jnp.exp(other_peak - top)
    return [
        top,
        own[1] * scale + other[1].astype(F32) * other_scale,
        own[2] * scale + other[2].astype(F32) * other_scale,
    ]


def thirds(message):
    size = message.shape[0] // 3
    return [message[k * size : (k + 1) * size] for k in range(3)]


def kernel_call(body, outs, scratch, flops, *operands, spaces=None, results=pltpu.VMEM):
    moved = sum(o.size * o.dtype.itemsize for o in operands)
    return pl.pallas_call(
        body,
        out_shape=outs,
        in_specs=[pl.BlockSpec(memory_space=m) for m in spaces or [pltpu.VMEM] * len(operands)],
        out_specs=jax.tree.map(lambda _: pl.BlockSpec(memory_space=results), outs),
        scratch_shapes=scratch,
        compiler_params=pltpu.CompilerParams(vmem_limit_bytes=14 * 1024 * 1024),
        cost_estimate=pl.CostEstimate(flops=flops, bytes_accessed=moved, transcendentals=0),
    )(*operands)


def on_device(
    others,
    axis,
    voxels,
    prior,
    conv_first,
    conv_second,
    score_x,
    score_y,
    plane_yz_w,
    plane_xz_w,
    norm_gain,
    mlp_in,
    mlp_out,
):
    rows, across, depth, channels = voxels.shape
    devices = lax.axis_size(axis)
    if rows != 2 or devices & (devices - 1) or devices < 16 or across % 8:
        raise ValueError("unsupported mesh")
    index = lax.axis_index(axis)
    half, quarter = across // 2, across // 4
    w_first = conv_first.reshape(3, 9, channels, channels)
    w_second = conv_second.reshape(3, 9, channels, channels)
    flops = 2 * voxels.size * channels * 27

    def beyond_edge(at):
        return at + 2 * (at % 2) - 1

    parts = lax.axis_size(others)
    pairs = []
    for base in range(0, parts * devices, devices):
        twin = base ^ devices if (base ^ devices) < parts * devices else base
        pairs += [(base, twin), (base + devices - 1, twin + devices - 1)]
        for i in range(base + 1, base + devices - 1, 2):
            pairs += [(i, i + 1), (i + 1, i)]
    cut = jax.ShapeDtypeStruct((rows, 2, quarter + 4, depth, channels), BF)
    cuts = kernel_call(
        functools.partial(cut_kernel, axis),
        (cut, cut),
        [pltpu.SemaphoreType.DMA((2, 2))],
        flops,
        voxels,
        spaces=(pltpu.HBM,),
    )
    far0 = lax.ppermute(cuts[0], (others, axis), pairs)
    far1 = lax.ppermute(cuts[1], (others, axis), pairs)
    near = swap(voxels, axis, 1)
    prior = prior.swapaxes(1, 2)
    edge, part = kernel_call(
        functools.partial(first_kernel, axis),
        (
            jax.ShapeDtypeStruct((rows, across + 2, depth, channels), F32),
            jax.ShapeDtypeStruct(voxels.shape, F32),
        ),
        [
            pltpu.VMEM((4, across + 2, depth, channels), BF),
            pltpu.VMEM((2, across + 2, depth, channels), BF),
        ],
        2 * flops,
        voxels,
        near,
        w_first,
        w_second,
    )

    def half_call(second, far, *state):
        feature = jax.ShapeDtypeStruct((rows, half, depth, channels), BF)
        message = jax.ShapeDtypeStruct((3 * quarter + 2 * second, depth, channels), BF)
        keep = jax.ShapeDtypeStruct((3, quarter, depth, channels), F32)
        strip = (jax.ShapeDtypeStruct((rows, depth, channels), BF),) if second else ()
        return kernel_call(
            functools.partial(half_kernel, axis, second),
            (feature, message, keep) + strip,
            [
                pltpu.VMEM((2, 2, quarter + 8, depth, channels), BF),
                pltpu.VMEM((2, 2, quarter + 2, depth, channels), BF),
            ],
            3 * flops // 4,
            edge,
            part,
            far,
            w_first,
            w_second,
            score_x,
            score_y,
            prior,
            *state,
        )

    masks = [1 << bit for bit in range(devices.bit_length() - 1)]
    early, message, keep = half_call(False, far0)
    got = swap(message, axis, masks[0])
    sent = jnp.concatenate([p.astype(BF) for p in merge(keep, thirds(got))])
    sent, early_first = lax.optimization_barrier((sent, early))
    arriving = swap(sent, axis, masks[1], masks[2])
    late, message, keep, strip = half_call(True, far1, early_first)
    got = swap(message, axis, masks[0])
    beyond = got[3 * quarter]
    carried = [got[3 * quarter + 1]]
    parts = merge(merge(keep, thirds(got[: 3 * quarter])), thirds(arriving))
    side = index % 2
    ahead, after = jnp.where(side == 0, 2, 4), jnp.where(side == 0, 4, 2)
    for mask in masks[2:]:
        if mask != masks[-1]:
            size = parts[0].shape[0] // 2
            upper = (index // (after if mask == masks[2] else mask)) % 2
            sent = [lax.dynamic_slice_in_dim(p, (1 - upper) * size, size, 0) for p in parts]
            parts = [lax.dynamic_slice_in_dim(p, upper * size, size, 0) for p in parts]
        else:
            sent = parts
        message = jnp.concatenate([p.astype(BF) for p in sent] + [carried[-1][None]], axis=0)
        got = swap(message, axis, mask, masks[1] if mask == masks[2] else mask)
        carried.append(got[-1])
        last_row = carried[-1]
        parts = merge(parts, thirds(got[:-1]))
        parts[0], carried[-1] = lax.optimization_barrier((parts[0], last_row))
    pooled = (parts[2] / parts[1]).astype(BF)
    for mask in reversed(masks[2:-1]):
        other = swap(pooled, axis, mask, masks[1] if mask == masks[2] else mask)
        pooled = jnp.concatenate([pooled, other], axis=0)
    other = index ^ ahead
    path = other ^ beyond_edge(other)
    row = carried[0]
    for k, value in enumerate(carried[1:]):
        row = jnp.where(path == (1 << (k + 3)) - 1, value, row)
    got = swap(jnp.concatenate([pooled, row[None]], axis=0), axis, masks[1], masks[2])
    direct = (side == 1) & (index ^ beyond_edge(index) == 3)
    before = jnp.where(direct, carried[1], got[-1])
    before = jnp.where((index == 0) | (index == devices - 1), jnp.zeros_like(row), before)
    pooled = jnp.concatenate([pooled, got[:-1]], axis=0)
    pooled = jnp.concatenate([pooled, swap(pooled, axis, masks[0])], axis=0)
    strip = jnp.concatenate([before[None], strip, beyond[None]], axis=0)
    return kernel_call(
        functools.partial(last_kernel, axis),
        jax.ShapeDtypeStruct(voxels.shape, BF),
        [
            pltpu.VMEM((across + 2, depth, channels), BF),
            pltpu.VMEM((rows, depth, channels), F32),
            pltpu.VMEM((rows, 4, quarter, depth, channels), BF),
            pltpu.SemaphoreType.DMA((rows, 4)),
        ],
        flops // 4,
        early,
        late,
        pooled,
        strip,
        plane_yz_w.reshape(3, 3, channels, channels),
        plane_xz_w.reshape(3, 3, channels, channels),
        norm_gain.reshape(1, channels),
        mlp_in,
        mlp_out,
        results=pl.ANY,
    )


def solution(mesh):
    spread = ("scene", "gx")
    return jax.shard_map(
        functools.partial(on_device, "scene", "gx"),
        mesh=mesh,
        in_specs=(P(spread, None, None, None), P(spread, None, None)) + (P(),) * 9,
        out_specs=P(spread, None, None, None),
        check_vma=False,
    )
```

```python
import functools

import jax
import jax.numpy as jnp
from jax import lax
from jax.experimental import pallas as pl
from jax.experimental.pallas import tpu as pltpu
from jax.sharding import PartitionSpec as P

BF = jnp.bfloat16
F32 = jnp.float32
PAIR = ({0: 0, 1: 1, 2: 2}, {1: 0, 2: 1, 3: 2})
LOWER = ({0: 0, 1: 1}, {1: 0})
UPPER = ({2: 2}, {2: 1, 3: 2})


SLOPE = 0.7978845608028654
BEND = SLOPE * 0.044715


def twice_activate(values):
    return values + values * jnp.tanh(values * (SLOPE + BEND * (values * values)))


def activate(values):
    return 0.5 * twice_activate(values)


def beside(blocks):
    return jnp.concatenate(blocks, axis=1)


def shift_depth(before, same, after, shape):
    depth = shape[1]
    place = lax.broadcasted_iota(jnp.int32, shape, 1)
    before = jnp.where(place == 0, 0.0, pltpu.roll(before.reshape(shape), 1, 1))
    after = jnp.where(place == depth - 1, 0.0, pltpu.roll(after.reshape(shape), depth - 1, 1))
    return before + same.reshape(shape) + after


def conv_rows(rows_ref, w_ref, taps, start, span, uses, names=None):
    depth, channels = rows_ref.shape[2:]
    shape = (span, depth, channels)
    zero = jnp.zeros((channels, channels), BF)
    windows = {
        r: [
            rows_ref[names[r] if names else r, pl.ds(start + b, span)].reshape(-1, channels)
            for b in range(3)
        ]
        for r in sorted(set(uses[0]) | set(uses[1]))
    }

    def weight(out, row, b, c):
        return w_ref[taps[uses[out][row]], 3 * b + c] if row in uses[out] else zero

    def product(left, right):
        rows = sorted(set(uses[left[0]]) | set(uses[right[0]]))
        lhs = beside([windows[r][b] for r in rows for b in range(3)])
        rhs = jnp.concatenate(
            [
                beside([weight(left[0], r, b, left[1]), weight(right[0], r, b, right[1])])
                for r in rows
                for b in range(3)
            ],
            axis=0,
        )
        total = jnp.dot(lhs, rhs, preferred_element_type=F32)
        return total[:, :channels], total[:, channels:]

    low0, low1 = product((0, 0), (0, 1))
    low2, high0 = product((0, 2), (1, 0))
    high1, high2 = product((1, 1), (1, 2))
    return shift_depth(low0, low1, low2, shape), shift_depth(high0, high1, high2, shape)


def clear_ends(rows_ref, width):
    rows, length, depth, channels = rows_ref.shape
    blank = jnp.zeros((width, depth, channels), rows_ref.dtype)
    for row in range(rows):
        rows_ref[row, :width] = blank
        rows_ref[row, length - width :] = blank


def cut_kernel(axis, own_ref, first_ref, second_ref, sems):
    half = own_ref.shape[1] // 2
    kept = lax.rem(lax.axis_index(axis) // 2, 2)
    fetches = []
    for k, (at, target) in enumerate(((kept, first_ref), (1 - kept, second_ref))):
        place = pl.ds(at * (half - 2), half + 2)
        fetches.append(pltpu.make_async_copy(own_ref.at[:, place], target, sems.at[k]))
    for fetch in fetches:
        fetch.start()
    for fetch in fetches:
        fetch.wait()


def first_kernel(axis, cut0_ref, cut1_ref, near_ref, w1_ref, w2_ref, edge_ref, part_ref, rows_ref, mid_ref):
    across = near_ref.shape[1]
    span = across // 2
    index = lax.axis_index(axis)
    side = lax.rem(index, 2)
    kept = lax.rem(index // 2, 2)
    clear_ends(rows_ref, 1)
    clear_ends(mid_ref, 1)
    clear_ends(edge_ref, 1)
    for row, at in enumerate((side, 1 - side)):
        rows_ref[row, pl.ds(1 + kept * (span - 2), span + 2)] = cut0_ref[at]
        rows_ref[row, pl.ds(1 + (1 - kept) * (span - 2), span + 2)] = cut1_ref[at]
        rows_ref[2 + row, 1 : across + 1] = near_ref[at]
    taps = (2 * side, 1, 2 - 2 * side)
    back = (2 - 2 * side, 1, 2 * side)
    for step in range(2):
        start = step * span
        low, high = conv_rows(rows_ref, w1_ref, taps, start, span, PAIR)
        mid_ref[0, 1 + start : 1 + start + span] = activate(low).astype(BF)
        mid_ref[1, 1 + start : 1 + start + span] = activate(high).astype(BF)
        low, high = conv_rows(rows_ref, w1_ref, back, start, span, LOWER, {0: 1, 1: 0})
        edge_ref[0, 1 + start : 1 + start + span] = low
        edge_ref[1, 1 + start : 1 + start + span] = high
    for step in range(2):
        start = step * span
        low, high = conv_rows(mid_ref, w2_ref, taps, start, span, UPPER, {2: 0, 3: 1})
        for u, part in enumerate((low, high)):
            own = rows_ref[u, 1 + start : 1 + start + span].astype(F32)
            part_ref[u, start : start + span] = part + own


def half_kernel(axis, second, *refs):
    edge_ref, part_ref, far_ref, w1_ref, w2_ref, x_ref, y_ref, prior_ref = refs[:8]
    if second:
        early_ref, feature_ref, message_ref, keep_ref, strip_ref, rows_ref, mid_ref = refs[8:]
    else:
        feature_ref, message_ref, keep_ref, rows_ref, mid_ref = refs[8:]
    across, depth, channels = part_ref.shape[1:]
    devices = lax.axis_size(axis)
    index = lax.axis_index(axis)
    side = lax.rem(index, 2)
    span = across // 2
    kept = lax.rem(index // 2, 2)
    half = kept if second else 1 - kept
    clear_ends(rows_ref, 2)
    local = pl.ds(2 - 2 * half, span + 2)
    border = jnp.logical_or(index == 0, index == devices - 1)
    blank = jnp.zeros((span + 2, depth, channels), BF)
    rows_ref[0, local] = jnp.where(border, blank, far_ref[1 - side])
    rows_ref[1, local] = jnp.where(border, blank, far_ref[side])
    back = (2 - 2 * side, 1, 2 * side)
    low, high = conv_rows(rows_ref, w1_ref, back, 0, span + 2, UPPER, {2: 0, 3: 1})
    inside = jnp.where(border, 0.0, 1.0)
    around = pl.ds(half * span, span + 2)
    mid_ref[1] = activate(low + edge_ref[0, around]).astype(BF)
    mid_ref[0] = (activate(high + edge_ref[1, around]) * inside).astype(BF)
    blank = jnp.zeros((depth, channels), BF)
    mid_ref[0, half * (span + 1)] = blank
    mid_ref[1, half * (span + 1)] = blank
    outs = conv_rows(mid_ref, w2_ref, (2 * side, 1, 2 - 2 * side), 0, span, LOWER)
    place = pl.ds(half * span, span)
    across_score, along_score = x_ref[...], y_ref[...]

    def prior_of(at, half):
        columns = prior_ref[at]
        columns = jnp.where(half == 0, columns[:, :span], columns[:, span:])
        return jnp.stack(
            [jnp.broadcast_to(columns[:, y : y + 1], (depth, channels)) for y in range(span)]
        )

    logits, features = [], []
    for u in range(2):
        at = side if u == 0 else 1 - side
        feature = (outs[u] + part_ref[u, place]).astype(BF)
        feature_ref[at] = feature
        prior = prior_of(at, half)
        if not second:
            logit = jnp.dot(feature.reshape(-1, channels), across_score, preferred_element_type=F32)
        else:
            score = beside([across_score, along_score])
            both = jnp.dot(feature.reshape(-1, channels), score, preferred_element_type=F32)
            logit = both[:, :channels]
            logit_y = both[:, channels:].reshape(span, depth, channels) + prior
            other = early_ref[at]
            other_y = jnp.dot(other.reshape(-1, channels), along_score, preferred_element_type=F32)
            other_y = other_y.reshape(span, depth, channels) + prior_of(at, 1 - half)
            top = jnp.maximum(jnp.max(logit_y, axis=0), jnp.max(other_y, axis=0))
            weights, others = jnp.exp(logit_y - top), jnp.exp(other_y - top)
            norm_sum = jnp.sum(weights, axis=0) + jnp.sum(others, axis=0)
            weighted = jnp.sum(weights * feature.astype(F32), axis=0)
            weighted = weighted + jnp.sum(others * other.astype(F32), axis=0)
            pooled = (weighted / norm_sum).astype(BF)
            strip_ref[u] = pooled
            message_ref[3 * (span // 2) + 1 - u] = pooled
        features.append(feature.astype(F32))
        logits.append(logit.reshape(span, depth, channels) + prior)
    peak = jnp.maximum(logits[0], logits[1])
    coarse = peak.astype(BF)
    shift = jnp.exp(jnp.clip(peak - coarse.astype(F32), -60.0, 60.0))
    low, high = jnp.exp(logits[0] - peak) * shift, jnp.exp(logits[1] - peak) * shift
    parts = (coarse.astype(F32), low + high, low * features[0] + high * features[1])
    quarter = span // 2
    for piece in range(2):
        cut = slice(piece * quarter, (piece + 1) * quarter)

        @pl.when(side == piece)
        def _():
            for k, part in enumerate(parts):
                keep_ref[k] = part[cut]

        @pl.when(side != piece)
        def _():
            for k, part in enumerate(parts):
                message_ref[k * quarter : (k + 1) * quarter] = part[cut].astype(BF)


def last_kernel(
    axis,
    early_ref,
    late_ref,
    pooled_ref,
    strip_ref,
    yz_ref,
    xz_ref,
    gain_ref,
    in_ref,
    out_w_ref,
    out_hbm,
    plane_ref,
    mix_ref,
    out_ref,
    sems,
):
    rows, half, depth, channels = early_ref.shape
    across = 2 * half
    index = lax.axis_index(axis)
    side = lax.rem(index, 2)
    kept = lax.rem(index // 2, 2)
    bits = lax.axis_size(axis).bit_length() - 2
    block = across >> bits
    order = [1, 0] + list(range(2, bits))
    mine = 0
    for bit in order:
        mine = mine * 2 + lax.rem(index // (1 << bit), 2)
    blank = jnp.zeros((depth, channels), BF)
    plane_ref[0] = blank
    plane_ref[across + 1] = blank
    for k in range(1 << bits):
        other = 0
        for bit in order:
            other = other * 2 + (k >> (bits - 1 - bit)) % 2
        place = jnp.bitwise_xor(mine, other)
        plane_ref[pl.ds(1 + place * block, block)] = pooled_ref[k * block : (k + 1) * block]

    def plane_product(windows, weights, shape):
        lhs = beside(windows)
        rhs = jnp.concatenate([beside(w) for w in weights], axis=0)
        total = jnp.dot(lhs, rhs, preferred_element_type=F32)
        parts = [total[:, c * channels : (c + 1) * channels] for c in range(3)]
        return shift_depth(*parts, shape).astype(BF).astype(F32)

    taps = (2 * side, 1, 2 - 2 * side)
    strip = strip_ref[...]
    mixed = plane_product(
        [strip[a : a + rows].reshape(-1, channels) for a in range(3)],
        [[xz_ref[taps[a], c] for c in range(3)] for a in range(3)],
        (rows, depth, channels),
    )
    mix_ref[side] = mixed[0]
    mix_ref[1 - side] = mixed[1]
    gain = gain_ref[...]
    span = out_ref.shape[2]
    copies = []
    for step in range(across // span):
        early = step * span < half
        feature_ref = early_ref if early else late_ref
        at = step * span % half
        start = (1 - kept if early else kept) * half + at
        plane = plane_product(
            [plane_ref[pl.ds(start + b, span)].reshape(-1, channels) for b in range(3)],
            [[yz_ref[b, c] for c in range(3)] for b in range(3)],
            (span, depth, channels),
        )
        feature = feature_ref[:, at : at + span].astype(F32)
        mixing = plane[None] + jnp.stack([mix_ref[row] for row in range(rows)])[:, None]
        joined = (feature * mixing).reshape(-1, channels)
        mean = jnp.mean(joined * joined, axis=-1, keepdims=True)
        normed = (joined * lax.rsqrt(mean + 1e-06) * gain).astype(BF)
        hidden = jnp.dot(normed, in_ref[...], preferred_element_type=F32)
        hidden = twice_activate(hidden).astype(BF)
        update = 0.5 * jnp.dot(hidden, out_w_ref[...], preferred_element_type=F32)
        encoded = (joined + update).astype(BF).reshape(rows, span, depth, channels)
        for row in range(rows):
            out_ref[row, step] = encoded[row]
            copies.append(
                pltpu.make_async_copy(
                    out_ref.at[row, step], out_hbm.at[row, pl.ds(start, span)], sems.at[row, step]
                )
            )
            copies[-1].start()
    for copy in copies:
        copy.wait()


def swap(values, axis, mask):
    devices = lax.axis_size(axis)
    return lax.ppermute(values, axis, [(i, i ^ mask) for i in range(devices)])


def merge(own, other):
    peak, other_peak = own[0], other[0].astype(F32)
    top = jnp.maximum(peak, other_peak)
    scale = jnp.exp(peak - top)
    other_scale = jnp.exp(other_peak - top)
    return [
        top,
        own[1] * scale + other[1].astype(F32) * other_scale,
        own[2] * scale + other[2].astype(F32) * other_scale,
    ]


def thirds(message):
    size = message.shape[0] // 3
    return [message[k * size : (k + 1) * size] for k in range(3)]


def kernel_call(body, outs, scratch, flops, *operands, spaces=None, results=pltpu.VMEM):
    moved = sum(o.size * o.dtype.itemsize for o in operands)
    return pl.pallas_call(
        body,
        out_shape=outs,
        in_specs=[pl.BlockSpec(memory_space=m) for m in spaces or [pltpu.VMEM] * len(operands)],
        out_specs=jax.tree.map(lambda _: pl.BlockSpec(memory_space=results), outs),
        scratch_shapes=scratch,
        compiler_params=pltpu.CompilerParams(vmem_limit_bytes=14 * 1024 * 1024),
        cost_estimate=pl.CostEstimate(flops=flops, bytes_accessed=moved, transcendentals=0),
    )(*operands)


def on_device(
    others,
    axis,
    voxels,
    prior,
    conv_first,
    conv_second,
    score_x,
    score_y,
    plane_yz_w,
    plane_xz_w,
    norm_gain,
    mlp_in,
    mlp_out,
):
    rows, across, depth, channels = voxels.shape
    devices = lax.axis_size(axis)
    if rows != 2 or devices & (devices - 1) or devices < 8:
        raise ValueError("unsupported mesh")
    index = lax.axis_index(axis)
    half, quarter = across // 2, across // 4
    w_first = conv_first.reshape(3, 9, channels, channels)
    w_second = conv_second.reshape(3, 9, channels, channels)
    flops = 2 * voxels.size * channels * 27

    def beyond_edge(at):
        return at + 2 * (at % 2) - 1

    parts = lax.axis_size(others)
    pairs = []
    for base in range(0, parts * devices, devices):
        twin = base ^ devices if (base ^ devices) < parts * devices else base
        pairs += [(base, twin), (base + devices - 1, twin + devices - 1)]
        for i in range(base + 1, base + devices - 1, 2):
            pairs += [(i, i + 1), (i + 1, i)]
    cut = jax.ShapeDtypeStruct((rows, half + 2, depth, channels), BF)
    cuts = kernel_call(
        functools.partial(cut_kernel, axis),
        (cut, cut),
        [pltpu.SemaphoreType.DMA((2,))],
        flops,
        voxels,
        spaces=(pltpu.HBM,),
    )
    far0 = lax.ppermute(cuts[0], (others, axis), pairs)
    far1 = lax.ppermute(cuts[1], (others, axis), pairs)
    near = swap(voxels, axis, 1)
    prior = prior.swapaxes(1, 2)
    edge, part = kernel_call(
        functools.partial(first_kernel, axis),
        (
            jax.ShapeDtypeStruct((rows, across + 2, depth, channels), F32),
            jax.ShapeDtypeStruct(voxels.shape, F32),
        ),
        [
            pltpu.VMEM((4, across + 2, depth, channels), BF),
            pltpu.VMEM((2, across + 2, depth, channels), BF),
        ],
        2 * flops,
        *cuts,
        near,
        w_first,
        w_second,
    )

    def half_call(second, far, *state):
        feature = jax.ShapeDtypeStruct((rows, half, depth, channels), BF)
        message = jax.ShapeDtypeStruct((3 * quarter + 2 * second, depth, channels), BF)
        keep = jax.ShapeDtypeStruct((3, quarter, depth, channels), F32)
        strip = (jax.ShapeDtypeStruct((rows, depth, channels), BF),) if second else ()
        return kernel_call(
            functools.partial(half_kernel, axis, second),
            (feature, message, keep) + strip,
            [
                pltpu.VMEM((2, half + 4, depth, channels), BF),
                pltpu.VMEM((2, half + 2, depth, channels), BF),
            ],
            3 * flops // 4,
            edge,
            part,
            far,
            w_first,
            w_second,
            score_x,
            score_y,
            prior,
            *state,
        )

    masks = [1 << bit for bit in range(devices.bit_length() - 1)]
    early, message, keep = half_call(False, far0)
    got = swap(message, axis, masks[0])
    sent = jnp.concatenate([p.astype(BF) for p in merge(keep, thirds(got))])
    sent, early_first = lax.optimization_barrier((sent, early))
    arriving = swap(sent, axis, masks[1])
    late, message, keep, strip = half_call(True, far1, early_first)
    got = swap(message, axis, masks[0])
    beyond = got[3 * quarter]
    carried = [got[3 * quarter + 1]]
    parts = merge(merge(keep, thirds(got[: 3 * quarter])), thirds(arriving))
    for mask in masks[2:]:
        if mask != masks[-1]:
            size = parts[0].shape[0] // 2
            upper = (index // mask) % 2
            sent = [lax.dynamic_slice_in_dim(p, (1 - upper) * size, size, 0) for p in parts]
            parts = [lax.dynamic_slice_in_dim(p, upper * size, size, 0) for p in parts]
        else:
            sent = parts
        message = jnp.concatenate([p.astype(BF) for p in sent] + [carried[-1][None]], axis=0)
        got = swap(message, axis, mask)
        carried.append(got[-1])
        last_row = carried[-1]
        parts = merge(parts, thirds(got[:-1]))
        parts[0], carried[-1] = lax.optimization_barrier((parts[0], last_row))
    pooled = (parts[2] / parts[1]).astype(BF)
    for mask in reversed(masks[2:-1]):
        pooled = jnp.concatenate([pooled, swap(pooled, axis, mask)], axis=0)
    other = index ^ masks[1]
    path = other ^ beyond_edge(other)
    row = carried[0]
    for k, value in enumerate(carried[1:]):
        row = jnp.where(path == (1 << (k + 3)) - 1, value, row)
    got = swap(jnp.concatenate([pooled, row[None]], axis=0), axis, masks[1])
    before = jnp.where((index == 0) | (index == devices - 1), jnp.zeros_like(row), got[-1])
    pooled = jnp.concatenate([pooled, got[:-1]], axis=0)
    pooled = jnp.concatenate([pooled, swap(pooled, axis, masks[0])], axis=0)
    strip = jnp.concatenate([before[None], strip, beyond[None]], axis=0)
    span = min(64, half)
    return kernel_call(
        functools.partial(last_kernel, axis),
        jax.ShapeDtypeStruct(voxels.shape, BF),
        [
            pltpu.VMEM((across + 2, depth, channels), BF),
            pltpu.VMEM((rows, depth, channels), F32),
            pltpu.VMEM((rows, across // span, span, depth, channels), BF),
            pltpu.SemaphoreType.DMA((rows, across // span)),
        ],
        flops // 4,
        early,
        late,
        pooled,
        strip,
        plane_yz_w.reshape(3, 3, channels, channels),
        plane_xz_w.reshape(3, 3, channels, channels),
        norm_gain.reshape(1, channels),
        mlp_in,
        mlp_out,
        results=pl.ANY,
    )


def solution(mesh):
    spread = ("scene", "gx")
    return jax.shard_map(
        functools.partial(on_device, "scene", "gx"),
        mesh=mesh,
        in_specs=(P(spread, None, None, None), P(spread, None, None)) + (P(),) * 9,
        out_specs=P(spread, None, None, None),
        check_vma=False,
    )
```

```python
import functools

import jax
import jax.numpy as jnp
from jax import lax
from jax.experimental import pallas as pl
from jax.experimental.pallas import tpu as pltpu
from jax.sharding import PartitionSpec as P

BF = jnp.bfloat16
F32 = jnp.float32
PAIR = ({0: 0, 1: 1, 2: 2}, {1: 0, 2: 1, 3: 2})
LOWER = ({0: 0, 1: 1}, {1: 0})
UPPER = ({2: 2}, {2: 1, 3: 2})


SLOPE = 0.7978845608028654
BEND = SLOPE * 0.044715


def twice_activate(values):
    return values + values * jnp.tanh(values * (SLOPE + BEND * (values * values)))


def activate(values):
    return 0.5 * twice_activate(values)


def beside(blocks):
    return jnp.concatenate(blocks, axis=1)


def shift_depth(before, same, after, shape):
    depth = shape[1]
    place = lax.broadcasted_iota(jnp.int32, shape, 1)
    before = jnp.where(place == 0, 0.0, pltpu.roll(before.reshape(shape), 1, 1))
    after = jnp.where(place == depth - 1, 0.0, pltpu.roll(after.reshape(shape), depth - 1, 1))
    return before + same.reshape(shape) + after


def conv_rows(rows_ref, w_ref, taps, start, span, uses, names=None):
    depth, channels = rows_ref.shape[2:]
    shape = (span, depth, channels)
    zero = jnp.zeros((channels, channels), BF)
    windows = {
        r: [
            rows_ref[names[r] if names else r, pl.ds(start + b, span)].reshape(-1, channels)
            for b in range(3)
        ]
        for r in sorted(set(uses[0]) | set(uses[1]))
    }

    def weight(out, row, b, c):
        return w_ref[taps[uses[out][row]], 3 * b + c] if row in uses[out] else zero

    def product(left, right):
        rows = sorted(set(uses[left[0]]) | set(uses[right[0]]))
        lhs = beside([windows[r][b] for r in rows for b in range(3)])
        rhs = jnp.concatenate(
            [
                beside([weight(left[0], r, b, left[1]), weight(right[0], r, b, right[1])])
                for r in rows
                for b in range(3)
            ],
            axis=0,
        )
        total = jnp.dot(lhs, rhs, preferred_element_type=F32)
        return total[:, :channels], total[:, channels:]

    low0, low1 = product((0, 0), (0, 1))
    low2, high0 = product((0, 2), (1, 0))
    high1, high2 = product((1, 1), (1, 2))
    return shift_depth(low0, low1, low2, shape), shift_depth(high0, high1, high2, shape)


def clear_ends(rows_ref, width):
    rows, length, depth, channels = rows_ref.shape
    blank = jnp.zeros((width, depth, channels), rows_ref.dtype)
    for row in range(rows):
        rows_ref[row, :width] = blank
        rows_ref[row, length - width :] = blank


def cut_kernel(axis, own_ref, first_ref, second_ref, sems):
    half = own_ref.shape[1] // 2
    kept = lax.rem(lax.axis_index(axis) // 2, 2)
    fetches = []
    for k, (at, target) in enumerate(((kept, first_ref), (1 - kept, second_ref))):
        place = pl.ds(at * (half - 2), half + 2)
        fetches.append(pltpu.make_async_copy(own_ref.at[:, place], target, sems.at[k]))
    for fetch in fetches:
        fetch.start()
    for fetch in fetches:
        fetch.wait()


def first_kernel(axis, cut0_ref, cut1_ref, near_ref, w1_ref, w2_ref, edge_ref, part_ref, rows_ref, mid_ref):
    across = near_ref.shape[1]
    span = across // 2
    index = lax.axis_index(axis)
    side = lax.rem(index, 2)
    kept = lax.rem(index // 2, 2)
    clear_ends(rows_ref, 1)
    clear_ends(mid_ref, 1)
    clear_ends(edge_ref, 1)
    for row, at in enumerate((side, 1 - side)):
        rows_ref[row, pl.ds(1 + kept * (span - 2), span + 2)] = cut0_ref[at]
        rows_ref[row, pl.ds(1 + (1 - kept) * (span - 2), span + 2)] = cut1_ref[at]
        rows_ref[2 + row, 1 : across + 1] = near_ref[at]
    taps = (2 * side, 1, 2 - 2 * side)
    back = (2 - 2 * side, 1, 2 * side)
    for step in range(2):
        start = step * span
        low, high = conv_rows(rows_ref, w1_ref, taps, start, span, PAIR)
        mid_ref[0, 1 + start : 1 + start + span] = activate(low).astype(BF)
        mid_ref[1, 1 + start : 1 + start + span] = activate(high).astype(BF)
        low, high = conv_rows(rows_ref, w1_ref, back, start, span, LOWER, {0: 1, 1: 0})
        edge_ref[0, 1 + start : 1 + start + span] = low
        edge_ref[1, 1 + start : 1 + start + span] = high
    for step in range(2):
        start = step * span
        low, high = conv_rows(mid_ref, w2_ref, taps, start, span, UPPER, {2: 0, 3: 1})
        for u, part in enumerate((low, high)):
            own = rows_ref[u, 1 + start : 1 + start + span].astype(F32)
            part_ref[u, start : start + span] = part + own


def half_kernel(axis, second, *refs):
    edge_ref, part_ref, far_ref, w1_ref, w2_ref, x_ref, y_ref, prior_ref = refs[:8]
    if second:
        early_ref, feature_ref, message_ref, keep_ref, strip_ref, rows_ref, mid_ref = refs[8:]
    else:
        feature_ref, message_ref, keep_ref, rows_ref, mid_ref = refs[8:]
    across, depth, channels = part_ref.shape[1:]
    devices = lax.axis_size(axis)
    index = lax.axis_index(axis)
    side = lax.rem(index, 2)
    span = across // 2
    kept = lax.rem(index // 2, 2)
    half = kept if second else 1 - kept
    clear_ends(rows_ref, 2)
    local = pl.ds(2 - 2 * half, span + 2)
    border = jnp.logical_or(index == 0, index == devices - 1)
    blank = jnp.zeros((span + 2, depth, channels), BF)
    rows_ref[0, local] = jnp.where(border, blank, far_ref[1 - side])
    rows_ref[1, local] = jnp.where(border, blank, far_ref[side])
    back = (2 - 2 * side, 1, 2 * side)
    low, high = conv_rows(rows_ref, w1_ref, back, 0, span + 2, UPPER, {2: 0, 3: 1})
    inside = jnp.where(border, 0.0, 1.0)
    around = pl.ds(half * span, span + 2)
    mid_ref[1] = activate(low + edge_ref[0, around]).astype(BF)
    mid_ref[0] = (activate(high + edge_ref[1, around]) * inside).astype(BF)
    blank = jnp.zeros((depth, channels), BF)
    mid_ref[0, half * (span + 1)] = blank
    mid_ref[1, half * (span + 1)] = blank
    outs = conv_rows(mid_ref, w2_ref, (2 * side, 1, 2 - 2 * side), 0, span, LOWER)
    place = pl.ds(half * span, span)
    across_score, along_score = x_ref[...], y_ref[...]

    def prior_of(at, half):
        columns = prior_ref[at]
        columns = jnp.where(half == 0, columns[:, :span], columns[:, span:])
        return jnp.stack(
            [jnp.broadcast_to(columns[:, y : y + 1], (depth, channels)) for y in range(span)]
        )

    logits, features = [], []
    for u in range(2):
        at = side if u == 0 else 1 - side
        feature = (outs[u] + part_ref[u, place]).astype(BF)
        feature_ref[at] = feature
        prior = prior_of(at, half)
        if not second:
            logit = jnp.dot(feature.reshape(-1, channels), across_score, preferred_element_type=F32)
        else:
            score = beside([across_score, along_score])
            both = jnp.dot(feature.reshape(-1, channels), score, preferred_element_type=F32)
            logit = both[:, :channels]
            logit_y = both[:, channels:].reshape(span, depth, channels) + prior
            other = early_ref[at]
            other_y = jnp.dot(other.reshape(-1, channels), along_score, preferred_element_type=F32)
            other_y = other_y.reshape(span, depth, channels) + prior_of(at, 1 - half)
            top = jnp.maximum(jnp.max(logit_y, axis=0), jnp.max(other_y, axis=0))
            weights, others = jnp.exp(logit_y - top), jnp.exp(other_y - top)
            norm_sum = jnp.sum(weights, axis=0) + jnp.sum(others, axis=0)
            weighted = jnp.sum(weights * feature.astype(F32), axis=0)
            weighted = weighted + jnp.sum(others * other.astype(F32), axis=0)
            pooled = (weighted / norm_sum).astype(BF)
            strip_ref[u] = pooled
            message_ref[3 * (span // 2) + 1 - u] = pooled
        features.append(feature.astype(F32))
        logits.append(logit.reshape(span, depth, channels) + prior)
    peak = jnp.maximum(logits[0], logits[1])
    coarse = peak.astype(BF)
    shift = jnp.exp(jnp.clip(peak - coarse.astype(F32), -60.0, 60.0))
    low, high = jnp.exp(logits[0] - peak) * shift, jnp.exp(logits[1] - peak) * shift
    parts = (coarse.astype(F32), low + high, low * features[0] + high * features[1])
    quarter = span // 2
    for piece in range(2):
        cut = slice(piece * quarter, (piece + 1) * quarter)

        @pl.when(side == piece)
        def _():
            for k, part in enumerate(parts):
                keep_ref[k] = part[cut]

        @pl.when(side != piece)
        def _():
            for k, part in enumerate(parts):
                message_ref[k * quarter : (k + 1) * quarter] = part[cut].astype(BF)


def last_kernel(axis, second, *refs):
    if second:
        feature_ref, done_ref, mix_ref, pooled_ref, yz_ref, gain_ref, in_ref, out_w_ref = refs[:8]
        out_hbm, plane_ref, out_ref, sems = refs[8:]
        across = feature_ref.shape[1]
    else:
        early_ref, late_ref, strip_ref, xz_ref, pooled_ref, yz_ref, gain_ref, in_ref, out_w_ref = refs[:9]
        feature_ref, out_ref, mix_ref, plane_ref = refs[9:]
        across = 2 * early_ref.shape[1]
    rows, (depth, channels) = feature_ref.shape[0], feature_ref.shape[2:]
    half, quarter, span = across // 2, across // 4, out_ref.shape[2]
    index = lax.axis_index(axis)
    side = lax.rem(index, 2)
    kept = lax.rem(index // 2, 2)
    bits = lax.axis_size(axis).bit_length() - 2
    block = across >> bits
    order = [1, 0] + list(range(2, bits))
    mine = 0
    for bit in order:
        mine = mine * 2 + lax.rem(index // (1 << bit), 2)
    copies = []
    if second:
        for row in range(rows):
            for h in range(2):
                place = pl.ds(h * half + side * quarter, quarter)
                copies.append(
                    pltpu.make_async_copy(
                        done_ref.at[row, h], out_hbm.at[row, place], sems.at[0, row, h]
                    )
                )
                copies[-1].start()
        blank = jnp.zeros((depth, channels), BF)
        plane_ref[0] = blank
        plane_ref[across + 1] = blank
    else:
        plane_ref[...] = jnp.zeros_like(plane_ref)
        feature_ref[:, pl.ds((1 - kept) * half, half)] = early_ref[...]
        feature_ref[:, pl.ds(kept * half, half)] = late_ref[...]
    for k in range(pooled_ref.shape[0] // block):
        other = 0
        for bit in order:
            other = other * 2 + (k >> (bits - 1 - bit)) % 2
        place = jnp.bitwise_xor(mine, other)
        plane_ref[pl.ds(1 + place * block, block)] = pooled_ref[k * block : (k + 1) * block]

    def plane_product(windows, weights, shape):
        lhs = beside(windows)
        rhs = jnp.concatenate([beside(w) for w in weights], axis=0)
        total = jnp.dot(lhs, rhs, preferred_element_type=F32)
        parts = [total[:, c * channels : (c + 1) * channels] for c in range(3)]
        return shift_depth(*parts, shape).astype(BF).astype(F32)

    if not second:
        taps = (2 * side, 1, 2 - 2 * side)
        strip = strip_ref[...]
        mixed = plane_product(
            [strip[a : a + rows].reshape(-1, channels) for a in range(3)],
            [[xz_ref[taps[a], c] for c in range(3)] for a in range(3)],
            (rows, depth, channels),
        )
        mix_ref[side] = mixed[0]
        mix_ref[1 - side] = mixed[1]
    if second:
        starts = [
            jnp.clip(h * half + (1 - side) * quarter - 1, 0, across - span) for h in range(2)
        ]
    else:
        starts = [h * half + side * quarter for h in range(2)]
    plane = plane_product(
        [
            jnp.concatenate([plane_ref[pl.ds(at + b, span)].reshape(-1, channels) for at in starts])
            for b in range(3)
        ],
        [[yz_ref[b, c] for c in range(3)] for b in range(3)],
        (2 * span, depth, channels),
    )
    feature = jnp.concatenate([feature_ref[:, pl.ds(at, span)] for at in starts], axis=1)
    mixing = plane[None] + jnp.stack([mix_ref[row] for row in range(rows)])[:, None]
    joined = (feature.astype(F32) * mixing).reshape(-1, channels)
    mean = jnp.mean(joined * joined, axis=-1, keepdims=True)
    normed = (joined * lax.rsqrt(mean + 1e-06) * gain_ref[...]).astype(BF)
    hidden = jnp.dot(normed, in_ref[...], preferred_element_type=F32)
    hidden = twice_activate(hidden).astype(BF)
    update = 0.5 * jnp.dot(hidden, out_w_ref[...], preferred_element_type=F32)
    encoded = (joined + update).astype(BF).reshape(rows, 2, span, depth, channels)
    for row in range(rows):
        for h in range(2):
            out_ref[row, h] = encoded[row, h]
    if second:
        for copy in copies:
            copy.wait()
        copies = []
        for row in range(rows):
            for h, at in enumerate(starts):
                copies.append(
                    pltpu.make_async_copy(
                        out_ref.at[row, h], out_hbm.at[row, pl.ds(at, span)], sems.at[1, row, h]
                    )
                )
                copies[-1].start()
        for copy in copies:
            copy.wait()


def swap(values, axis, mask):
    devices = lax.axis_size(axis)
    return lax.ppermute(values, axis, [(i, i ^ mask) for i in range(devices)])


def merge(own, other):
    peak, other_peak = own[0], other[0].astype(F32)
    top = jnp.maximum(peak, other_peak)
    scale = jnp.exp(peak - top)
    other_scale = jnp.exp(other_peak - top)
    return [
        top,
        own[1] * scale + other[1].astype(F32) * other_scale,
        own[2] * scale + other[2].astype(F32) * other_scale,
    ]


def thirds(message):
    size = message.shape[0] // 3
    return [message[k * size : (k + 1) * size] for k in range(3)]


def kernel_call(body, outs, scratch, flops, *operands, spaces=None, results=None):
    moved = sum(o.size * o.dtype.itemsize for o in operands)
    return pl.pallas_call(
        body,
        out_shape=outs,
        in_specs=[pl.BlockSpec(memory_space=m) for m in spaces or [pltpu.VMEM] * len(operands)],
        out_specs=jax.tree.map(
            lambda _, space: pl.BlockSpec(memory_space=space),
            outs,
            results or jax.tree.map(lambda _: pltpu.VMEM, outs),
        ),
        scratch_shapes=scratch,
        compiler_params=pltpu.CompilerParams(vmem_limit_bytes=14 * 1024 * 1024),
        cost_estimate=pl.CostEstimate(flops=flops, bytes_accessed=moved, transcendentals=0),
    )(*operands)


def on_device(
    others,
    axis,
    voxels,
    prior,
    conv_first,
    conv_second,
    score_x,
    score_y,
    plane_yz_w,
    plane_xz_w,
    norm_gain,
    mlp_in,
    mlp_out,
):
    rows, across, depth, channels = voxels.shape
    devices = lax.axis_size(axis)
    if rows != 2 or devices & (devices - 1) or devices < 8:
        raise ValueError("unsupported mesh")
    index = lax.axis_index(axis)
    half, quarter = across // 2, across // 4
    w_first = conv_first.reshape(3, 9, channels, channels)
    w_second = conv_second.reshape(3, 9, channels, channels)
    flops = 2 * voxels.size * channels * 27

    def beyond_edge(at):
        return at + 2 * (at % 2) - 1

    parts = lax.axis_size(others)
    pairs = []
    for base in range(0, parts * devices, devices):
        twin = base ^ devices if (base ^ devices) < parts * devices else base
        pairs += [(base, twin), (base + devices - 1, twin + devices - 1)]
        for i in range(base + 1, base + devices - 1, 2):
            pairs += [(i, i + 1), (i + 1, i)]
    cut = jax.ShapeDtypeStruct((rows, half + 2, depth, channels), BF)
    cuts = kernel_call(
        functools.partial(cut_kernel, axis),
        (cut, cut),
        [pltpu.SemaphoreType.DMA((2,))],
        flops,
        voxels,
        spaces=(pltpu.HBM,),
    )
    far0 = lax.ppermute(cuts[0], (others, axis), pairs)
    far1 = lax.ppermute(cuts[1], (others, axis), pairs)
    near = swap(voxels, axis, 1)
    prior = prior.swapaxes(1, 2)
    edge, part = kernel_call(
        functools.partial(first_kernel, axis),
        (
            jax.ShapeDtypeStruct((rows, across + 2, depth, channels), F32),
            jax.ShapeDtypeStruct(voxels.shape, F32),
        ),
        [
            pltpu.VMEM((4, across + 2, depth, channels), BF),
            pltpu.VMEM((2, across + 2, depth, channels), BF),
        ],
        2 * flops,
        *cuts,
        near,
        w_first,
        w_second,
    )

    def half_call(second, far, *state):
        feature = jax.ShapeDtypeStruct((rows, half, depth, channels), BF)
        message = jax.ShapeDtypeStruct((3 * quarter + 2 * second, depth, channels), BF)
        keep = jax.ShapeDtypeStruct((3, quarter, depth, channels), F32)
        strip = (jax.ShapeDtypeStruct((rows, depth, channels), BF),) if second else ()
        return kernel_call(
            functools.partial(half_kernel, axis, second),
            (feature, message, keep) + strip,
            [
                pltpu.VMEM((2, half + 4, depth, channels), BF),
                pltpu.VMEM((2, half + 2, depth, channels), BF),
            ],
            3 * flops // 4,
            edge,
            part,
            far,
            w_first,
            w_second,
            score_x,
            score_y,
            prior,
            *state,
        )

    masks = [1 << bit for bit in range(devices.bit_length() - 1)]
    early, message, keep = half_call(False, far0)
    got = swap(message, axis, masks[0])
    sent = jnp.concatenate([p.astype(BF) for p in merge(keep, thirds(got))])
    sent, early_first = lax.optimization_barrier((sent, early))
    arriving = swap(sent, axis, masks[1])
    late, message, keep, strip = half_call(True, far1, early_first)
    got = swap(message, axis, masks[0])
    beyond = got[3 * quarter]
    carried = [got[3 * quarter + 1]]
    parts = merge(merge(keep, thirds(got[: 3 * quarter])), thirds(arriving))
    for mask in masks[2:]:
        if mask != masks[-1]:
            size = parts[0].shape[0] // 2
            upper = (index // mask) % 2
            sent = [lax.dynamic_slice_in_dim(p, (1 - upper) * size, size, 0) for p in parts]
            parts = [lax.dynamic_slice_in_dim(p, upper * size, size, 0) for p in parts]
        else:
            sent = parts
        message = jnp.concatenate([p.astype(BF) for p in sent] + [carried[-1][None]], axis=0)
        got = swap(message, axis, mask)
        carried.append(got[-1])
        last_row = carried[-1]
        parts = merge(parts, thirds(got[:-1]))
        parts[0], carried[-1] = lax.optimization_barrier((parts[0], last_row))
    pooled = (parts[2] / parts[1]).astype(BF)
    for mask in reversed(masks[2:-1]):
        pooled = jnp.concatenate([pooled, swap(pooled, axis, mask)], axis=0)
    other = index ^ masks[1]
    path = other ^ beyond_edge(other)
    row = carried[0]
    for k, value in enumerate(carried[1:]):
        row = jnp.where(path == (1 << (k + 3)) - 1, value, row)
    got = swap(jnp.concatenate([pooled, row[None]], axis=0), axis, masks[1])
    before = jnp.where((index == 0) | (index == devices - 1), jnp.zeros_like(row), got[-1])
    pooled = jnp.concatenate([pooled, got[:-1]], axis=0)
    strip = jnp.concatenate([before[None], strip, beyond[None]], axis=0)
    weights = (
        plane_yz_w.reshape(3, 3, channels, channels),
        norm_gain.reshape(1, channels),
        mlp_in,
        mlp_out,
    )
    whole = jax.ShapeDtypeStruct(voxels.shape, BF)
    plane = pltpu.VMEM((across + 2, depth, channels), BF)
    other = swap(pooled, axis, masks[0])
    feature, done, mix = kernel_call(
        functools.partial(last_kernel, axis, False),
        (
            whole,
            jax.ShapeDtypeStruct((rows, 2, quarter, depth, channels), BF),
            jax.ShapeDtypeStruct((rows, depth, channels), F32),
        ),
        [plane],
        flops // 8,
        early,
        late,
        strip,
        plane_xz_w.reshape(3, 3, channels, channels),
        pooled,
        *weights,
    )
    return kernel_call(
        functools.partial(last_kernel, axis, True),
        whole,
        [
            plane,
            pltpu.VMEM((rows, 2, quarter + 2, depth, channels), BF),
            pltpu.SemaphoreType.DMA((2, rows, 2)),
        ],
        flops // 8,
        feature,
        done,
        mix,
        jnp.concatenate([pooled, other], axis=0),
        *weights,
        results=pltpu.HBM,
    )


def solution(mesh):
    spread = ("scene", "gx")
    return jax.shard_map(
        functools.partial(on_device, "scene", "gx"),
        mesh=mesh,
        in_specs=(P(spread, None, None, None), P(spread, None, None)) + (P(),) * 9,
        out_specs=P(spread, None, None, None),
        check_vma=False,
    )
```

```python
import functools

import jax
import jax.numpy as jnp
from jax import lax
from jax.experimental import pallas as pl
from jax.experimental.pallas import tpu as pltpu
from jax.sharding import PartitionSpec as P

BF = jnp.bfloat16
F32 = jnp.float32
PAIR = ({0: 0, 1: 1, 2: 2}, {1: 0, 2: 1, 3: 2})
LOWER = ({0: 0, 1: 1}, {1: 0})
UPPER = ({2: 2}, {2: 1, 3: 2})


SLOPE = 0.7978845608028654
BEND = SLOPE * 0.044715


def twice_activate(values):
    return values + values * jnp.tanh(values * (SLOPE + BEND * (values * values)))


def activate(values):
    return 0.5 * twice_activate(values)


def beside(blocks):
    return jnp.concatenate(blocks, axis=1)


def shift_depth(before, same, after, shape):
    depth = shape[1]
    place = lax.broadcasted_iota(jnp.int32, shape, 1)
    before = jnp.where(place == 0, 0.0, pltpu.roll(before.reshape(shape), 1, 1))
    after = jnp.where(place == depth - 1, 0.0, pltpu.roll(after.reshape(shape), depth - 1, 1))
    return before + same.reshape(shape) + after


def conv_rows(rows_ref, w_ref, taps, start, span, uses, names=None):
    depth, channels = rows_ref.shape[2:]
    shape = (span, depth, channels)
    zero = jnp.zeros((channels, channels), BF)
    windows = {
        r: [
            rows_ref[names[r] if names else r, pl.ds(start + b, span)].reshape(-1, channels)
            for b in range(3)
        ]
        for r in sorted(set(uses[0]) | set(uses[1]))
    }

    def weight(out, row, b, c):
        return w_ref[taps[uses[out][row]], 3 * b + c] if row in uses[out] else zero

    def product(left, right):
        rows = sorted(set(uses[left[0]]) | set(uses[right[0]]))
        lhs = beside([windows[r][b] for r in rows for b in range(3)])
        rhs = jnp.concatenate(
            [
                beside([weight(left[0], r, b, left[1]), weight(right[0], r, b, right[1])])
                for r in rows
                for b in range(3)
            ],
            axis=0,
        )
        total = jnp.dot(lhs, rhs, preferred_element_type=F32)
        return total[:, :channels], total[:, channels:]

    low0, low1 = product((0, 0), (0, 1))
    low2, high0 = product((0, 2), (1, 0))
    high1, high2 = product((1, 1), (1, 2))
    return shift_depth(low0, low1, low2, shape), shift_depth(high0, high1, high2, shape)


def clear_ends(rows_ref, width):
    rows, length, depth, channels = rows_ref.shape
    blank = jnp.zeros((width, depth, channels), rows_ref.dtype)
    for row in range(rows):
        rows_ref[row, :width] = blank
        rows_ref[row, length - width :] = blank


def cut_kernel(axis, second, own_ref, cut_ref, sem):
    half = own_ref.shape[1] // 2
    kept = lax.rem(lax.axis_index(axis) // 2, 2)
    at = 1 - kept if second else kept
    fetch = pltpu.make_async_copy(own_ref.at[:, pl.ds(at * (half - 2), half + 2)], cut_ref, sem)
    fetch.start()
    fetch.wait()


def half_of(axis, second):
    kept = lax.rem(lax.axis_index(axis) // 2, 2)
    return kept if second else 1 - kept


def first_kernel(axis, second, own_ref, near_ref, w1_ref, w2_ref, edge_ref, part_ref, rows_ref, mid_ref):
    span, (depth, channels) = part_ref.shape[1], part_ref.shape[2:]
    side = lax.rem(lax.axis_index(axis), 2)
    half = half_of(axis, second)
    clear_ends(rows_ref, 2)
    inner = pl.ds(half * (span - 2), span + 2)
    local = pl.ds(2 - 2 * half, span + 2)
    for row, at in enumerate((side, 1 - side)):
        rows_ref[row, local] = own_ref[at]
        rows_ref[2 + row, local] = near_ref[at, inner]
    taps = (2 * side, 1, 2 - 2 * side)
    back = (2 - 2 * side, 1, 2 * side)
    low, high = conv_rows(rows_ref, w1_ref, taps, 0, span + 2, PAIR)
    mid_ref[0] = activate(low).astype(BF)
    mid_ref[1] = activate(high).astype(BF)
    blank = jnp.zeros((depth, channels), BF)
    mid_ref[0, half * (span + 1)] = blank
    mid_ref[1, half * (span + 1)] = blank
    low, high = conv_rows(rows_ref, w1_ref, back, 0, span + 2, LOWER, {0: 1, 1: 0})
    edge_ref[0] = low
    edge_ref[1] = high
    outs = conv_rows(mid_ref, w2_ref, taps, 0, span, UPPER, {2: 0, 3: 1})
    for u in range(2):
        part_ref[u] = outs[u] + rows_ref[u, 2 : 2 + span].astype(F32)


def half_kernel(axis, second, *refs):
    edge_ref, part_ref, far_ref, w1_ref, w2_ref, x_ref, y_ref, prior_ref = refs[:8]
    if second:
        early_ref, feature_ref, message_ref, keep_ref, strip_ref, rows_ref, mid_ref = refs[8:]
    else:
        feature_ref, message_ref, keep_ref, rows_ref, mid_ref = refs[8:]
    span, depth, channels = part_ref.shape[1:]
    devices = lax.axis_size(axis)
    index = lax.axis_index(axis)
    side = lax.rem(index, 2)
    half = half_of(axis, second)
    clear_ends(rows_ref, 2)
    local = pl.ds(2 - 2 * half, span + 2)
    border = jnp.logical_or(index == 0, index == devices - 1)
    blank = jnp.zeros((span + 2, depth, channels), BF)
    rows_ref[0, local] = jnp.where(border, blank, far_ref[1 - side])
    rows_ref[1, local] = jnp.where(border, blank, far_ref[side])
    back = (2 - 2 * side, 1, 2 * side)
    low, high = conv_rows(rows_ref, w1_ref, back, 0, span + 2, UPPER, {2: 0, 3: 1})
    inside = jnp.where(border, 0.0, 1.0)
    mid_ref[1] = activate(low + edge_ref[0]).astype(BF)
    mid_ref[0] = (activate(high + edge_ref[1]) * inside).astype(BF)
    blank = jnp.zeros((depth, channels), BF)
    mid_ref[0, half * (span + 1)] = blank
    mid_ref[1, half * (span + 1)] = blank
    outs = conv_rows(mid_ref, w2_ref, (2 * side, 1, 2 - 2 * side), 0, span, LOWER)
    across_score, along_score = x_ref[...], y_ref[...]

    def prior_of(at, half):
        columns = prior_ref[at]
        columns = jnp.where(half == 0, columns[:, :span], columns[:, span:])
        return jnp.stack(
            [jnp.broadcast_to(columns[:, y : y + 1], (depth, channels)) for y in range(span)]
        )

    logits, features = [], []
    for u in range(2):
        at = side if u == 0 else 1 - side
        feature = (outs[u] + part_ref[u]).astype(BF)
        feature_ref[at] = feature
        prior = prior_of(at, half)
        if not second:
            logit = jnp.dot(feature.reshape(-1, channels), across_score, preferred_element_type=F32)
        else:
            score = beside([across_score, along_score])
            both = jnp.dot(feature.reshape(-1, channels), score, preferred_element_type=F32)
            logit = both[:, :channels]
            logit_y = both[:, channels:].reshape(span, depth, channels) + prior
            other = early_ref[at]
            other_y = jnp.dot(other.reshape(-1, channels), along_score, preferred_element_type=F32)
            other_y = other_y.reshape(span, depth, channels) + prior_of(at, 1 - half)
            top = jnp.maximum(jnp.max(logit_y, axis=0), jnp.max(other_y, axis=0))
            weights, others = jnp.exp(logit_y - top), jnp.exp(other_y - top)
            norm_sum = jnp.sum(weights, axis=0) + jnp.sum(others, axis=0)
            weighted = jnp.sum(weights * feature.astype(F32), axis=0)
            weighted = weighted + jnp.sum(others * other.astype(F32), axis=0)
            pooled = (weighted / norm_sum).astype(BF)
            strip_ref[u] = pooled
            message_ref[3 * (span // 2) + 1 - u] = pooled
        features.append(feature.astype(F32))
        logits.append(logit.reshape(span, depth, channels) + prior)
    peak = jnp.maximum(logits[0], logits[1])
    coarse = peak.astype(BF)
    shift = jnp.exp(jnp.clip(peak - coarse.astype(F32), -60.0, 60.0))
    low, high = jnp.exp(logits[0] - peak) * shift, jnp.exp(logits[1] - peak) * shift
    parts = (coarse.astype(F32), low + high, low * features[0] + high * features[1])
    quarter = span // 2
    for piece in range(2):
        cut = slice(piece * quarter, (piece + 1) * quarter)

        @pl.when(side == piece)
        def _():
            for k, part in enumerate(parts):
                keep_ref[k] = part[cut]

        @pl.when(side != piece)
        def _():
            for k, part in enumerate(parts):
                message_ref[k * quarter : (k + 1) * quarter] = part[cut].astype(BF)


def last_kernel(axis, second, *refs):
    if second:
        feature_ref, done_ref, mix_ref, pooled_ref, yz_ref, gain_ref, in_ref, out_w_ref = refs[:8]
        out_hbm, plane_ref, out_ref, sems = refs[8:]
        across = feature_ref.shape[1]
    else:
        early_ref, late_ref, strip_ref, xz_ref, pooled_ref, yz_ref, gain_ref, in_ref, out_w_ref = refs[:9]
        feature_ref, out_ref, mix_ref, plane_ref = refs[9:]
        across = 2 * early_ref.shape[1]
    rows, (depth, channels) = feature_ref.shape[0], feature_ref.shape[2:]
    half, quarter, span = across // 2, across // 4, out_ref.shape[2]
    index = lax.axis_index(axis)
    side = lax.rem(index, 2)
    kept = lax.rem(index // 2, 2)
    bits = lax.axis_size(axis).bit_length() - 2
    block = across >> bits
    order = [1, 0] + list(range(2, bits))
    mine = 0
    for bit in order:
        mine = mine * 2 + lax.rem(index // (1 << bit), 2)
    copies = []
    if second:
        for row in range(rows):
            for h in range(2):
                place = pl.ds(h * half + side * quarter, quarter)
                copies.append(
                    pltpu.make_async_copy(
                        done_ref.at[row, h], out_hbm.at[row, place], sems.at[0, row, h]
                    )
                )
                copies[-1].start()
        blank = jnp.zeros((depth, channels), BF)
        plane_ref[0] = blank
        plane_ref[across + 1] = blank
    else:
        plane_ref[...] = jnp.zeros_like(plane_ref)
        feature_ref[:, pl.ds((1 - kept) * half, half)] = early_ref[...]
        feature_ref[:, pl.ds(kept * half, half)] = late_ref[...]
    for k in range(pooled_ref.shape[0] // block):
        other = 0
        for bit in order:
            other = other * 2 + (k >> (bits - 1 - bit)) % 2
        place = jnp.bitwise_xor(mine, other)
        plane_ref[pl.ds(1 + place * block, block)] = pooled_ref[k * block : (k + 1) * block]

    def plane_product(windows, weights, shape):
        lhs = beside(windows)
        rhs = jnp.concatenate([beside(w) for w in weights], axis=0)
        total = jnp.dot(lhs, rhs, preferred_element_type=F32)
        parts = [total[:, c * channels : (c + 1) * channels] for c in range(3)]
        return shift_depth(*parts, shape).astype(BF).astype(F32)

    if not second:
        taps = (2 * side, 1, 2 - 2 * side)
        strip = strip_ref[...]
        mixed = plane_product(
            [strip[a : a + rows].reshape(-1, channels) for a in range(3)],
            [[xz_ref[taps[a], c] for c in range(3)] for a in range(3)],
            (rows, depth, channels),
        )
        mix_ref[side] = mixed[0]
        mix_ref[1 - side] = mixed[1]
    if second:
        starts = [
            jnp.clip(h * half + (1 - side) * quarter - 1, 0, across - span) for h in range(2)
        ]
    else:
        starts = [h * half + side * quarter for h in range(2)]
    plane = plane_product(
        [
            jnp.concatenate([plane_ref[pl.ds(at + b, span)].reshape(-1, channels) for at in starts])
            for b in range(3)
        ],
        [[yz_ref[b, c] for c in range(3)] for b in range(3)],
        (2 * span, depth, channels),
    )
    feature = jnp.concatenate([feature_ref[:, pl.ds(at, span)] for at in starts], axis=1)
    mixing = plane[None] + jnp.stack([mix_ref[row] for row in range(rows)])[:, None]
    joined = (feature.astype(F32) * mixing).reshape(-1, channels)
    mean = jnp.mean(joined * joined, axis=-1, keepdims=True)
    normed = (joined * lax.rsqrt(mean + 1e-06) * gain_ref[...]).astype(BF)
    hidden = jnp.dot(normed, in_ref[...], preferred_element_type=F32)
    hidden = twice_activate(hidden).astype(BF)
    update = 0.5 * jnp.dot(hidden, out_w_ref[...], preferred_element_type=F32)
    encoded = (joined + update).astype(BF).reshape(rows, 2, span, depth, channels)
    for row in range(rows):
        for h in range(2):
            out_ref[row, h] = encoded[row, h]
    if second:
        for copy in copies:
            copy.wait()
        copies = []
        for row in range(rows):
            for h, at in enumerate(starts):
                copies.append(
                    pltpu.make_async_copy(
                        out_ref.at[row, h], out_hbm.at[row, pl.ds(at, span)], sems.at[1, row, h]
                    )
                )
                copies[-1].start()
        for copy in copies:
            copy.wait()


def swap(values, axis, mask):
    devices = lax.axis_size(axis)
    return lax.ppermute(values, axis, [(i, i ^ mask) for i in range(devices)])


def merge(own, other):
    peak, other_peak = own[0], other[0].astype(F32)
    top = jnp.maximum(peak, other_peak)
    scale = jnp.exp(peak - top)
    other_scale = jnp.exp(other_peak - top)
    return [
        top,
        own[1] * scale + other[1].astype(F32) * other_scale,
        own[2] * scale + other[2].astype(F32) * other_scale,
    ]


def thirds(message):
    size = message.shape[0] // 3
    return [message[k * size : (k + 1) * size] for k in range(3)]


def kernel_call(body, outs, scratch, flops, *operands, spaces=None, results=None):
    moved = sum(o.size * o.dtype.itemsize for o in operands)
    return pl.pallas_call(
        body,
        out_shape=outs,
        in_specs=[pl.BlockSpec(memory_space=m) for m in spaces or [pltpu.VMEM] * len(operands)],
        out_specs=jax.tree.map(
            lambda _, space: pl.BlockSpec(memory_space=space),
            outs,
            results or jax.tree.map(lambda _: pltpu.VMEM, outs),
        ),
        scratch_shapes=scratch,
        compiler_params=pltpu.CompilerParams(vmem_limit_bytes=14 * 1024 * 1024),
        cost_estimate=pl.CostEstimate(flops=flops, bytes_accessed=moved, transcendentals=0),
    )(*operands)


def on_device(
    others,
    axis,
    voxels,
    prior,
    conv_first,
    conv_second,
    score_x,
    score_y,
    plane_yz_w,
    plane_xz_w,
    norm_gain,
    mlp_in,
    mlp_out,
):
    rows, across, depth, channels = voxels.shape
    devices = lax.axis_size(axis)
    if rows != 2 or devices & (devices - 1) or devices < 8:
        raise ValueError("unsupported mesh")
    index = lax.axis_index(axis)
    half, quarter = across // 2, across // 4
    w_first = conv_first.reshape(3, 9, channels, channels)
    w_second = conv_second.reshape(3, 9, channels, channels)
    flops = 2 * voxels.size * channels * 27

    def beyond_edge(at):
        return at + 2 * (at % 2) - 1

    parts = lax.axis_size(others)
    pairs = []
    for base in range(0, parts * devices, devices):
        twin = base ^ devices if (base ^ devices) < parts * devices else base
        pairs += [(base, twin), (base + devices - 1, twin + devices - 1)]
        for i in range(base + 1, base + devices - 1, 2):
            pairs += [(i, i + 1), (i + 1, i)]
    cut = jax.ShapeDtypeStruct((rows, half + 2, depth, channels), BF)
    cuts = [
        kernel_call(
            functools.partial(cut_kernel, axis, second),
            cut,
            [pltpu.SemaphoreType.DMA],
            flops * second,
            voxels,
            spaces=(pltpu.HBM,),
        )
        for second in (False, True)
    ]
    far0 = lax.ppermute(cuts[0], (others, axis), pairs)
    far1 = lax.ppermute(cuts[1], (others, axis), pairs)
    near = swap(voxels, axis, 1)
    prior = prior.swapaxes(1, 2)

    def base_call(second, own):
        return kernel_call(
            functools.partial(first_kernel, axis, second),
            (
                jax.ShapeDtypeStruct((rows, half + 2, depth, channels), F32),
                jax.ShapeDtypeStruct((rows, half, depth, channels), F32),
            ),
            [
                pltpu.VMEM((4, half + 4, depth, channels), BF),
                pltpu.VMEM((2, half + 2, depth, channels), BF),
            ],
            flops,
            own,
            near,
            w_first,
            w_second,
        )

    def half_call(second, base, far, *state):
        feature = jax.ShapeDtypeStruct((rows, half, depth, channels), BF)
        message = jax.ShapeDtypeStruct((3 * quarter + 2 * second, depth, channels), BF)
        keep = jax.ShapeDtypeStruct((3, quarter, depth, channels), F32)
        strip = (jax.ShapeDtypeStruct((rows, depth, channels), BF),) if second else ()
        return kernel_call(
            functools.partial(half_kernel, axis, second),
            (feature, message, keep) + strip,
            [
                pltpu.VMEM((2, half + 4, depth, channels), BF),
                pltpu.VMEM((2, half + 2, depth, channels), BF),
            ],
            3 * flops // 4,
            *base,
            far,
            w_first,
            w_second,
            score_x,
            score_y,
            prior,
            *state,
        )

    masks = [1 << bit for bit in range(devices.bit_length() - 1)]
    base = base_call(False, cuts[1])
    early, message, keep = half_call(False, base, far0)
    got = swap(message, axis, masks[0])
    sent = jnp.concatenate([p.astype(BF) for p in merge(keep, thirds(got))])
    sent, early_first = lax.optimization_barrier((sent, early))
    arriving = swap(sent, axis, masks[1])
    base = base_call(True, cuts[0])
    late, message, keep, strip = half_call(True, base, far1, early_first)
    got = swap(message, axis, masks[0])
    beyond = got[3 * quarter]
    carried = [got[3 * quarter + 1]]
    parts = merge(merge(keep, thirds(got[: 3 * quarter])), thirds(arriving))
    for mask in masks[2:]:
        if mask != masks[-1]:
            size = parts[0].shape[0] // 2
            upper = (index // mask) % 2
            sent = [lax.dynamic_slice_in_dim(p, (1 - upper) * size, size, 0) for p in parts]
            parts = [lax.dynamic_slice_in_dim(p, upper * size, size, 0) for p in parts]
        else:
            sent = parts
        message = jnp.concatenate([p.astype(BF) for p in sent] + [carried[-1][None]], axis=0)
        got = swap(message, axis, mask)
        carried.append(got[-1])
        last_row = carried[-1]
        parts = merge(parts, thirds(got[:-1]))
        parts[0], carried[-1] = lax.optimization_barrier((parts[0], last_row))
    pooled = (parts[2] / parts[1]).astype(BF)
    for mask in reversed(masks[2:-1]):
        pooled = jnp.concatenate([pooled, swap(pooled, axis, mask)], axis=0)
    other = index ^ masks[1]
    path = other ^ beyond_edge(other)
    row = carried[0]
    for k, value in enumerate(carried[1:]):
        row = jnp.where(path == (1 << (k + 3)) - 1, value, row)
    got = swap(jnp.concatenate([pooled, row[None]], axis=0), axis, masks[1])
    before = jnp.where((index == 0) | (index == devices - 1), jnp.zeros_like(row), got[-1])
    pooled = jnp.concatenate([pooled, got[:-1]], axis=0)
    strip = jnp.concatenate([before[None], strip, beyond[None]], axis=0)
    weights = (
        plane_yz_w.reshape(3, 3, channels, channels),
        norm_gain.reshape(1, channels),
        mlp_in,
        mlp_out,
    )
    whole = jax.ShapeDtypeStruct(voxels.shape, BF)
    plane = pltpu.VMEM((across + 2, depth, channels), BF)
    other = swap(pooled, axis, masks[0])
    feature, done, mix = kernel_call(
        functools.partial(last_kernel, axis, False),
        (
            whole,
            jax.ShapeDtypeStruct((rows, 2, quarter, depth, channels), BF),
            jax.ShapeDtypeStruct((rows, depth, channels), F32),
        ),
        [plane],
        flops // 8,
        early,
        late,
        strip,
        plane_xz_w.reshape(3, 3, channels, channels),
        pooled,
        *weights,
    )
    return kernel_call(
        functools.partial(last_kernel, axis, True),
        whole,
        [
            plane,
            pltpu.VMEM((rows, 2, quarter + 2, depth, channels), BF),
            pltpu.SemaphoreType.DMA((2, rows, 2)),
        ],
        flops // 8,
        feature,
        done,
        mix,
        jnp.concatenate([pooled, other], axis=0),
        *weights,
        results=pltpu.HBM,
    )


def solution(mesh):
    spread = ("scene", "gx")
    return jax.shard_map(
        functools.partial(on_device, "scene", "gx"),
        mesh=mesh,
        in_specs=(P(spread, None, None, None), P(spread, None, None)) + (P(),) * 9,
        out_specs=P(spread, None, None, None),
        check_vma=False,
    )
```
